32 devices in a mesh: wide: 16 (over z, y, core), narrow: 2 (over x).
Axes of the slice: x: 2, y: 2, z: 4, core: 2. Of those that a mesh axis runs over, the one named last changes fastest.
Arguments:
- users: float32 [49152, 256], P(('wide', 'narrow')), may hold values from -1.5 to 1.5
- user_state: float32 [49152], P(('wide', 'narrow')), may hold values from 0.05 to 0.5
- items: float32 [8192, 256], P('wide'), may hold values from -1.5 to 1.5
- item_state: float32 [8192], P('wide'), may hold values from 0.05 to 0.5
- tile_ids: int32 [16, 2, 2, 16], P('wide', 'narrow'), may hold values from 0 to 47, as said below
- tile_count: int32 [16, 2, 2], P('wide', 'narrow'), may hold values from 1 to 16, as said below
- pos_items: int32 [16, 2, 2, 16, 128], P('wide', 'narrow'), may hold values from 0 to 127
- neg_offsets: int32 [16, 2, 2, 16], P('wide', 'narrow'), may hold values from 0 to 384
Outputs:
- new_users: float32 [49152, 256], P(('wide', 'narrow'))
- new_user_state: float32 [49152], P(('wide', 'narrow'))
- new_items: float32 [8192, 256], P('wide')
- new_item_state: float32 [8192], P('wide')
The draws below stay inside these ranges and needn't reach their ends.
Inputs may be any that keep to these rules, and one draw needn't show every extreme that they name: `tile_ids`: within one list the 16 ids are distinct tile numbers; slots at or after the count are ignored. `tile_count`: some entry equals 16.
All inputs are finite; a program needn't handle non-finite values.
Results may differ from the reference program's by a relative error of at most 0.0003.
Values sent between devices are 32-bit elements; how exact they have to be, the bound alone decides.
A program may use at most 64 MiB of HBM per device.

```python
import math
import jax
import jax.numpy as jnp
from jax import lax

K = 256
TILE = 128
U_DEV = 1536
ITEM_BLK = 512
TILES = 16
GROUP = 8
STRATA = 2
USERS = 49152
ITEMS = 8192
N_WIDE = 16
N_NARROW = 2


def draw_tile_ids(key, part):
    total = U_DEV // TILE * (ITEM_BLK // TILE)
    lists = N_WIDE * N_NARROW * STRATA
    keys = jax.random.split(jax.random.fold_in(key, 11), lists)
    chosen = jax.vmap(lambda single: jax.random.permutation(single, total)[:TILES])(keys)
    return chosen.reshape(N_WIDE, N_NARROW, STRATA, TILES).astype(jnp.int32)


def draw_tile_count(key, part):
    first = jax.random.randint(jax.random.fold_in(key, 21), (N_WIDE * N_NARROW * STRATA,), 0, TILES)
    second = jax.random.randint(jax.random.fold_in(key, 22), (N_WIDE * N_NARROW * STRATA,), 0, TILES)
    counts = 1 + first * second // TILES
    place = jax.random.randint(jax.random.fold_in(key, 23), (), 0, N_WIDE * N_NARROW * STRATA)
    counts = counts.at[place].set(TILES)
    return counts.reshape(N_WIDE, N_NARROW, STRATA).astype(jnp.int32)


def plant(drawn, key, low, largest):
    longest = drawn.shape.index(max(drawn.shape))
    spots = []
    for shift in (0, 1):
        where = [jax.random.randint(jax.random.fold_in(key, axis), (), 0, length) for axis, length in enumerate(drawn.shape)]
        where[longest] = (where[longest] + shift) % drawn.shape[longest]
        spots.append(tuple(where))
    return drawn.at[spots[0]].set(low).at[spots[1]].set(largest)


def levels(key, shape, cuts, low, top_value):
    def one(axis_at, shards_of):
        heights = jax.random.uniform(jax.random.fold_in(jax.random.fold_in(key, 6), axis_at), (shards_of,), jnp.float32, low / len(cuts), top_value / len(cuts))
        return jnp.repeat(jnp.exp(heights), shape[axis_at] // shards_of).reshape((-1,) + (1,) * (len(shape) - axis_at - 1))

    level = one(*cuts[0])
    for cut in cuts[1:]:
        level = level * one(*cut)
    return level


def noise(key, dims, spread, limit, pieces=(), held_as=jnp.bfloat16):
    drawn = jax.random.normal(key, dims, jnp.float32) * spread
    if len(pieces) > 0:
        drawn = levels(key, dims, pieces, -0.22, 0.18) * drawn
    return jnp.clip(drawn, min=-limit, max=limit).astype(held_as)


def setup_inputs(seed: int = 0) -> dict:
    splits = jax.random.split(jax.random.key(seed), 9)
    users = noise(splits[0], (USERS, K), 0.25, 1.5, ((0, 32),), jnp.float32)
    user_state = jnp.clip(jnp.exp(math.log(0.5) - 2.3025851 * jax.random.uniform(splits[1], (USERS,), jnp.float32) ** levels(splits[1], (USERS,), ((0, 32),), -0.2, 0.2)), 0.05, 0.5)
    items = noise(splits[2], (ITEMS, K), 0.25, 1.5, ((0, 16),), jnp.float32)
    item_state = jnp.clip(jnp.exp(math.log(0.5) - 2.3025851 * jax.random.uniform(splits[3], (ITEMS,), jnp.float32) ** levels(splits[3], (ITEMS,), ((0, 16),), -0.2, 0.2)), 0.05, 0.5)
    tile_ids = draw_tile_ids(jax.random.fold_in(splits[8], 71), 0)
    tile_count = draw_tile_count(jax.random.fold_in(splits[8], 71), 0)
    pos_items = plant(jax.random.randint(splits[6], (N_WIDE, N_NARROW, STRATA, TILES, TILE), 0, TILE), jax.random.fold_in(splits[6], 1), 0, TILE - 1).astype(jnp.int32)
    neg_offsets = plant(jax.random.randint(splits[7], (N_WIDE, N_NARROW, STRATA, TILES), 0, ITEM_BLK - TILE + 1), jax.random.fold_in(splits[7], 1), 0, ITEM_BLK - TILE).astype(jnp.int32)
    return {"users": users, "user_state": user_state, "items": items, "item_state": item_state, "tile_ids": tile_ids, "tile_count": tile_count, "pos_items": pos_items, "neg_offsets": neg_offsets}


highest = lax.Precision.HIGHEST
step_rate = 0.25

def adagrad(values, state, grad):
    new_state = state + lax.optimization_barrier(jnp.mean(grad * grad, axis=-1))
    return (values - step_rate * grad / jnp.sqrt(new_state)[..., None], new_state)

def group_update(carry, user_tiles, block_tiles, negatives, tile_list, positives, offsets, live):
    user_grad, pos_grad, neg_grad = carry
    row_count = user_tiles.shape[0]
    col_count = block_tiles.shape[0]
    side = user_tiles.shape[1]
    width = user_tiles.shape[2]
    lanes = jnp.arange(side, dtype=jnp.int32)
    row_index = (tile_list // col_count).astype(jnp.int32)
    col_index = (tile_list % col_count).astype(jnp.int32)
    factors = user_tiles[row_index]
    column_block = block_tiles[col_index]
    onehot = (positives[:, :, None] == lanes[None, None, :]).astype(jnp.float32)
    pos_rows = jnp.einsum('gui,gik->guk', onehot, column_block, precision=highest)
    neg_rows = jax.vmap(lambda start: lax.dynamic_slice_in_dim(negatives, start, side, 0))(offsets)
    pos_score = lax.optimization_barrier(jnp.sum(factors * pos_rows, axis=-1))
    neg_score = jnp.einsum('guk,gjk->guj', factors, neg_rows, precision=highest)
    coeffs = jax.nn.sigmoid(neg_score - pos_score[:, :, None]) * (live[:, None, None] / side)
    totals = lax.optimization_barrier(jnp.sum(coeffs, axis=-1))
    factor_grad = jnp.einsum('guj,gjk->guk', coeffs, neg_rows, precision=highest) - totals[:, :, None] * pos_rows
    positive_grad = -jnp.einsum('gui,guk->gik', onehot, totals[:, :, None] * factors, precision=highest)
    negative_grad = jnp.einsum('guj,guk->gjk', coeffs, factors, precision=highest)
    row_hot = (row_index[:, None] == jnp.arange(row_count, dtype=jnp.int32)[None, :]).astype(jnp.float32)
    col_hot = (col_index[:, None] == jnp.arange(col_count, dtype=jnp.int32)[None, :]).astype(jnp.float32)
    user_grad = user_grad + jnp.einsum('gr,guk->ruk', row_hot, factor_grad, precision=highest)
    pos_grad = pos_grad + jnp.einsum('gc,gik->cik', col_hot, positive_grad, precision=highest)
    neg_index = (offsets[:, None] + lanes[None, :]).reshape(-1)
    neg_grad = neg_grad.at[neg_index].add(negative_grad.reshape(-1, width))
    return (user_grad, pos_grad, neg_grad)

def device_grads(users, block, negatives, tile_list, count, positives, offsets):
    width = users.shape[1]
    user_tiles = users.reshape(-1, TILE, width)
    block_tiles = block.reshape(-1, TILE, width)
    groups = tile_list.shape[0] // GROUP
    slots = jnp.arange(tile_list.shape[0], dtype=jnp.int32)
    live = (slots < count).astype(jnp.float32)
    init = (jnp.zeros(user_tiles.shape, jnp.float32), jnp.zeros(block_tiles.shape, jnp.float32), jnp.zeros(block.shape, jnp.float32))

    def advance(carry, inputs):
        return (group_update(carry, user_tiles, block_tiles, negatives, inputs[0], inputs[1], inputs[2], inputs[3]), None)
    inputs = (tile_list.reshape(groups, GROUP), positives.reshape(groups, GROUP, TILE), offsets.reshape(groups, GROUP), live.reshape(groups, GROUP))
    carry, unused = lax.scan(advance, init, inputs)
    return (carry[0].reshape(users.shape), carry[1].reshape(block.shape), carry[2])

def reference(users, user_state, items, item_state, tile_ids, tile_count, pos_items, neg_offsets):
    wide_count = N_WIDE
    users_r = users.reshape(wide_count, N_NARROW, U_DEV, K)
    state_r = user_state.reshape(wide_count, N_NARROW, U_DEV)
    blocks = items.reshape(wide_count, ITEM_BLK, K)
    block_state = item_state.reshape(wide_count, ITEM_BLK)
    for stratum in range(STRATA):
        current = jnp.roll(blocks, stratum, 0)
        opposite = jnp.roll(current, wide_count // 2, 0)

        def one_position(index, current=current, opposite=opposite, users_r=users_r, state_r=state_r, stratum=stratum):
            grads = jax.vmap(device_grads, in_axes=(0, None, None, 0, 0, 0, 0))(users_r[index], current[index], opposite[index], tile_ids[index, :, stratum], tile_count[index, :, stratum], pos_items[index, :, stratum], neg_offsets[index, :, stratum])
            fresh_users, fresh_state = adagrad(users_r[index], state_r[index], grads[0])
            return (fresh_users, fresh_state, lax.optimization_barrier(jnp.sum(grads[1], axis=0)), lax.optimization_barrier(jnp.sum(grads[2], axis=0)))
        users_r, state_r, pos_sum, neg_sum = lax.map(one_position, jnp.arange(wide_count, dtype=jnp.int32))
        total = pos_sum + jnp.roll(neg_sum, wide_count // 2, 0)
        by_block = jnp.roll(total, -stratum, 0)
        blocks, block_state = adagrad(blocks, block_state, by_block)
    return (users_r.reshape(-1, K), state_r.reshape(-1), blocks.reshape(-1, K), block_state.reshape(-1))
```

```python
import functools

import jax
import jax.numpy as jnp
from jax import lax
from jax.experimental import pallas as pl
from jax.experimental.pallas import tpu as pltpu
from jax.sharding import PartitionSpec as P

TILE = 128
STRATA = 2
BATCH = 4
GROUPS = 4
CHUNKS = 8
LANES = 4
LAG_POS = 3
LAG_NEG = 4
WINDOW = TILE + 16
MESH = pl.DeviceIdType.MESH
step_rate = 0.25
f32 = jnp.float32
bf16 = jnp.bfloat16
VMEM = pltpu.MemorySpace.VMEM
SMEM = pltpu.MemorySpace.SMEM


def dot(a, b, dims):
    return lax.dot_general(a, b, (dims, ((), ())), preferred_element_type=f32)


def pair(x):
    high = x.astype(bf16)
    low = (x - high.astype(f32)).astype(bf16)
    return jnp.concatenate([high, low], axis=0)


def tiles_kernel(
    stratum, ids, count, offsets, positives, users, state, block, negatives,
    new_users, new_state, pos_grad, neg_grad, split, square, padded, spread,
):
    cols = block.shape[0] // TILE
    rows = users.shape[0] // TILE
    side = TILE
    width = users.shape[1]
    new_users[...] = jnp.zeros(new_users.shape, f32)
    pos_grad[...] = jnp.zeros(pos_grad.shape, f32)
    spread[...] = jnp.zeros(spread.shape, f32)
    length = negatives.shape[0]
    padded[0:length, :] = negatives[...]
    padded[length:, :] = jnp.zeros((padded.shape[0] - length, width), f32)
    for col in range(cols):
        split[col] = pair(block[col * side : (col + 1) * side, :])
    live_count = count[0, stratum]
    item = lax.broadcasted_iota(jnp.int32, (side, side), 0)
    place = lax.broadcasted_iota(jnp.int32, (side, WINDOW), 1)

    def batch(step, carry):
        work = []
        for lane in range(BATCH):
            slot = step * BATCH + lane
            tile = ids[stratum, slot]
            within = lax.rem(offsets[stratum, slot], 8)
            window = pl.ds(pl.multiple_of(offsets[stratum, slot] - within, 8), WINDOW)
            row = pl.multiple_of(lax.div(tile, cols) * side, side)
            col = lax.rem(tile, cols)
            live = jnp.where(slot < live_count, 1.0 / side, 0.0).astype(f32)
            factors = users[pl.ds(row, side), :]
            factors_low = factors.astype(bf16)
            neg_rows = padded[window, :].astype(bf16)
            hot = jnp.where(item == positives[stratum, pl.ds(slot, 1), :], 1.0, 0.0).astype(f32)
            hot_t = hot.T.astype(bf16)
            hot = hot.astype(bf16)
            pos_rows = dot(jnp.concatenate([hot_t, hot_t], axis=1), split[col], ((1,), (0,)))
            neg_score = dot(factors_low, neg_rows, ((1,), (1,)))
            pos_score = jnp.sum(factors * pos_rows, axis=-1, keepdims=True)
            chosen = jnp.logical_and(place >= within, place < within + side)
            coeffs = jnp.where(chosen, live, 0.0) / (1.0 + jnp.exp(pos_score - neg_score))
            totals = jnp.sum(coeffs, axis=-1, keepdims=True)
            coeffs_low = coeffs.astype(bf16)
            factor_grad = dot(coeffs_low, neg_rows, ((1,), (0,))) - totals * pos_rows
            positive = dot(
                jnp.concatenate([hot, hot], axis=1), pair(totals * factors), ((1,), (0,))
            )
            coeffs_t = coeffs.T.astype(bf16)
            negative = dot(
                jnp.concatenate([coeffs_t, coeffs_t], axis=1), pair(factors), ((1,), (0,))
            )
            work.append((row, col, window, factor_grad, positive, negative))
        for row, col, window, factor_grad, positive, negative in work:
            new_users[pl.ds(row, side), :] += factor_grad
            at = pl.ds(pl.multiple_of(col * side, side), side)
            pos_grad[at, :] -= positive
            spread[window, :] += negative
        return carry

    lax.fori_loop(0, lax.div(live_count + (BATCH - 1), BATCH), batch, 0)
    neg_grad[...] = spread[0:length, :]
    square[...] = jnp.zeros(square.shape, f32)
    square[0:rows, :] = state[...]
    sums = square[...].T
    for row in range(rows):
        at = slice(row * side, (row + 1) * side)
        grad = new_users[at, :]
        fresh = sums[:, row : row + 1] + jnp.sum(grad * grad, axis=-1, keepdims=True) * (1.0 / width)
        new_users[at, :] = users[at, :] - (step_rate / jnp.sqrt(fresh)) * grad
        square[:, row : row + 1] = fresh
    new_state[...] = square[...].T[0:rows, :]


def run_tiles(stratum, ids, count, offsets, positives, users, state, block, negatives):
    width = users.shape[1]
    cols = block.shape[0] // TILE
    return pl.pallas_call(
        functools.partial(tiles_kernel, stratum),
        out_shape=(
            jax.ShapeDtypeStruct(users.shape, f32),
            jax.ShapeDtypeStruct(state.shape, f32),
            jax.ShapeDtypeStruct(block.shape, f32),
            jax.ShapeDtypeStruct(block.shape, f32),
        ),
        in_specs=[pl.BlockSpec(memory_space=SMEM)] * 3 + [pl.BlockSpec(memory_space=VMEM)] * 5,
        out_specs=(pl.BlockSpec(memory_space=VMEM),) * 4,
        scratch_shapes=[
            pltpu.VMEM((cols, 2 * TILE, width), bf16),
            pltpu.VMEM((TILE, TILE), f32),
            pltpu.VMEM((block.shape[0] + 16, width), f32),
            pltpu.VMEM((block.shape[0] + 16, width), f32),
        ],
        compiler_params=pltpu.CompilerParams(vmem_limit_bytes=24 * 1024 * 1024),
        name="tiles",
    )(ids, count, offsets, positives, users, state, block, negatives)


def greet(devices):
    barrier = pltpu.get_barrier_semaphore()
    for device in devices:
        pl.semaphore_signal(barrier, inc=1, device_id=device, device_id_type=MESH)
    pl.semaphore_wait(barrier, len(devices))


def start_remote(src, dst, sems, kind, chunk, device):
    copy = pltpu.make_async_remote_copy(
        src_ref=src,
        dst_ref=dst,
        send_sem=sems.at[0, kind, chunk],
        recv_sem=sems.at[1, kind, chunk],
        device_id=device,
        device_id_type=MESH,
    )
    copy.start()
    return copy


def whole_kernel(
    wide, users_hbm, user_state_hbm, items_hbm, item_state_hbm, ids_hbm, positives_hbm, count_hbm,
    offsets_hbm,
    new_users, new_user_state, new_items, new_item_state,
    users, high, low, user_state, block, block_next, item_state, positives, split, negs, negs_low,
    coeffs, pos_rows, neg_grad, beside_neg, summed, far, pos_grad, beside_pos, pos_sum, home_pos,
    fresh, factor_grad, hot_t, square, user_sums, item_sums, scores, totals, partial,
    ids, count, offsets, slot_of, sems, local_sems,
):
    w, r = lax.axis_index("wide"), lax.axis_index("narrow")
    slots = ids.shape[1]
    rows, side, width = users.shape
    cols = block.shape[0] // side
    half = block.shape[0] // 2
    size = half // CHUNKS
    per = CHUNKS // GROUPS
    quarter = half // GROUPS

    def at(shift):
        return (lax.rem(w + shift + wide, wide), r)

    across, ahead, behind = at(wide // 2), at(1), at(-1)
    far_ahead, far_behind = at(wide // 2 + 1), at(wide // 2 - 1)
    beside = (w, 1 - r)
    greet([beside, across, ahead, behind, far_ahead, far_behind])

    def span(which, chunk):
        return pl.ds(pl.multiple_of(which * half + chunk * size, size), size)

    def inner(which, chunk):
        return pl.ds(pl.multiple_of(which * quarter + (chunk % per) * size, size), size)

    def local(chunk):
        return slice(chunk * size, (chunk + 1) * size)

    started = []

    def send(src, dst, kind, chunk, device):
        copy = start_remote(src, dst, sems, kind, chunk, device)
        started.append(copy)
        return copy

    def neg_at(stratum, which, chunk):
        return negs.at[stratum, chunk // per, inner(which, chunk), :]

    arriving = [
        send(items_hbm.at[span(r, c), :], neg_at(0, r, c), 0, c, across) for c in range(CHUNKS)
    ]
    loads = []
    for k, (src, dst) in enumerate(
        [
            (ids_hbm, ids), (count_hbm, count), (offsets_hbm, offsets), (positives_hbm, positives),
            (items_hbm, block), (users_hbm, users), (user_state_hbm, user_state),
            (item_state_hbm, item_state),
        ]
    ):
        loads.append(pltpu.make_async_copy(src, dst, local_sems.at[k]))
        loads[-1].start()
    factor_grad[slots] = jnp.zeros((side, width), f32)
    square[...] = jnp.zeros(square.shape, f32)
    for load in loads:
        load.wait()

    item = lax.broadcasted_iota(jnp.int32, (side, side), 0)
    lane = lax.broadcasted_iota(jnp.int32, (side, side), 1)

    def find(tile, carry):
        for stratum in range(STRATA):
            found = jnp.int32(slots)
            for slot in range(slots):
                found = jnp.where(ids[stratum, slot] == tile, jnp.int32(slot), found)
            slot_of[stratum, tile] = found
        return carry

    lax.fori_loop(0, rows * cols, find, 0)

    def hots(stratum):
        def step(slot, carry):
            hot = jnp.where(item == positives[stratum, pl.ds(slot, 1), :], 1.0, 0.0).astype(f32)
            hot_t[stratum, slot] = hot.T.astype(bf16)
            return carry

        lax.fori_loop(0, slots, step, 0)

    def split_users(source):
        def step(row, carry):
            value = source[row]
            top = value.astype(bf16)
            high[row] = top
            low[row] = (value - top.astype(f32)).astype(bf16)
            return carry

        lax.fori_loop(0, rows, step, 0)

    def row_at(stratum, slot):
        return lax.div(ids[stratum, slot], cols)

    def prepare(stratum, source, own):
        for col in range(cols):
            split[col] = pair(own[col * side : (col + 1) * side, :])

        def step(batch, columns):
            for j in range(LANES):
                slot = batch * LANES + j
                hot = hot_t[stratum, slot]
                picked = dot(
                    jnp.concatenate([hot, hot], axis=1),
                    split[lax.rem(ids[stratum, slot], cols)],
                    ((1,), (0,)),
                )
                pos_rows[slot] = picked
                score = jnp.sum(source[row_at(stratum, slot)] * picked, axis=-1, keepdims=True)
                columns = jnp.where(lane == slot, score, columns)
            return columns

        columns = lax.fori_loop(0, slots // LANES, step, jnp.zeros((side, side), f32))
        scores[...] = columns.T
        partial[...] = jnp.zeros(partial.shape, f32)

    def group(stratum, g):
        near = negs[stratum, g].astype(bf16)
        here = slice(g * side, (g + 1) * side)
        negs_low[here, :] = near
        index = item + jnp.where(item >= quarter, half - quarter, 0) + g * quarter

        def step(batch, carry):
            weights, tops, lows = [], [], []
            for j in range(LANES):
                slot = batch * LANES + j
                top = high[row_at(stratum, slot)]
                live = jnp.where(slot < count[0, stratum], 1.0 / side, 0.0).astype(f32)
                score = dot(near, top, ((1,), (1,)))
                place = index - offsets[stratum, slot]
                chosen = jnp.logical_and(place >= 0, place < side)
                part = jnp.where(chosen, live, 0.0) / (
                    1.0 + jnp.exp(scores[pl.ds(slot, 1), :] - score)
                )
                partial[slot] += jnp.sum(part.reshape(side // 8, 8, side), axis=0)
                part = part.astype(bf16)
                coeffs[slot, here, :] = part
                weights.append(part)
                tops.append(top)
                lows.append(low[row_at(stratum, slot)])
            left = jnp.concatenate(weights, axis=1)
            total = dot(left, jnp.concatenate(tops, axis=0), ((1,), (0,)))
            total += dot(left, jnp.concatenate(lows, axis=0), ((1,), (0,)))
            return carry + total

        neg_grad[stratum, g] = lax.fori_loop(
            0, slots // LANES, step, jnp.zeros((side, width), f32)
        )

    def add_totals():
        square[0:slots, :] = jnp.sum(partial[...], axis=1)
        totals[...] = square[...].T

    def positive(stratum, which):
        where = lax.broadcasted_iota(jnp.int32, (half, side), 0) + which * half

        def step(slot, carry):
            wanted = positives[stratum, pl.ds(slot, 1), :] + lax.rem(ids[stratum, slot], cols) * side
            hot = jnp.where(where == wanted, square[pl.ds(slot, 1), :], 0.0)
            top = hot.astype(bf16)
            rest = (hot - top.astype(f32)).astype(bf16)
            upper = high[row_at(stratum, slot)]
            lower = low[row_at(stratum, slot)]
            total = dot(
                jnp.concatenate([top, rest], axis=1),
                jnp.concatenate([upper, upper], axis=0),
                ((1,), (0,)),
            )
            return carry - total - dot(top, lower, ((1,), (0,)))

        begin = pl.ds(pl.multiple_of(which * half, half), half)
        pos_grad[stratum, begin, :] = lax.fori_loop(
            0, slots, step, jnp.zeros((half, width), f32)
        )

    def factor_part(slot):
        factor_grad[slot] = (
            dot(coeffs[slot], negs_low[...], ((0,), (0,)))
            - totals[:, slot : slot + 1] * pos_rows[slot]
        )

    def update_part(stratum, row, source, last):
        grad = factor_grad[slot_of[stratum, row * cols]]
        for col in range(1, cols):
            grad += factor_grad[slot_of[stratum, row * cols + col]]
        sums = user_sums[:, row : row + 1] + jnp.sum(grad * grad, axis=-1, keepdims=True) * (
            1.0 / width
        )
        value = source[row] - (step_rate / jnp.sqrt(sums)) * grad
        user_sums[:, row : row + 1] = sums
        new_users[row] = value
        if not last:
            top = value.astype(bf16)
            high[row] = top
            low[row] = (value - top.astype(f32)).astype(bf16)

    def user_work(stratum, source, last):
        for slot in range(slots):
            yield functools.partial(factor_part, slot)
        for row in range(rows):
            yield functools.partial(update_part, stratum, row, source, last)

    def adagrad(stratum, c, grad, value):
        col, begin = c * size // side, c * size % side
        sums = item_sums[begin : begin + size, col : col + 1] + jnp.sum(
            grad * grad, axis=-1, keepdims=True
        ) * (1.0 / width)
        item_sums[begin : begin + size, col : col + 1] = sums
        return value - (step_rate / jnp.sqrt(sums)) * grad

    square[0:rows, :] = user_state[...]
    user_sums[...] = square[...].T
    square[0 : half // side, :] = item_state[r]
    item_sums[...] = square[...].T
    for stratum in range(STRATA):
        hots(stratum)
    split_users(users)
    prepare(0, users, block)

    def chunks_of(g):
        return range(g * per, (g + 1) * per)

    def work_through(stratum, arriving, relayed, kind, target):
        side_neg, out = [], []

        def relay(c):
            arriving[c].wait_recv()
            relayed.append(send(neg_at(stratum, r, c), neg_at(stratum, r, c), kind, c, beside))

        def add(g):
            for c in chunks_of(g):
                side_neg[c].wait_recv()
                summed[stratum, local(c), :] = (
                    neg_grad[stratum, g, inner(r, c), :] + beside_neg[stratum, local(c), :]
                )
                out.append(
                    send(
                        summed.at[stratum, local(c), :], far.at[stratum, local(c), :],
                        kind + 2, c, target,
                    )
                )

        for g in range(GROUPS):
            for c in range(len(relayed), (g + 1) * per):
                relay(c)
            for c in chunks_of(g):
                relayed[c].wait_recv()
            if g + 1 < GROUPS:
                for c in range(len(relayed), (g + 2) * per):
                    relay(c)
            group(stratum, g)
            for c in chunks_of(g):
                side_neg.append(
                    send(
                        neg_grad.at[stratum, g, inner(1 - r, c), :],
                        beside_neg.at[stratum, local(c), :],
                        kind + 1, c, beside,
                    )
                )
            if g > 0:
                add(g - 1)
        add_totals()
        positive(stratum, 1 - r)
        side_pos = [
            send(
                pos_grad.at[stratum, span(1 - r, c), :], beside_pos.at[stratum, local(c), :],
                kind + 3, c, beside,
            )
            for c in range(CHUNKS)
        ]
        add(GROUPS - 1)
        positive(stratum, r)
        return out, side_pos

    out, side_pos = work_through(0, arriving, [], 1, across)
    work = list(user_work(0, users, False))
    pieces = CHUNKS + LAG_POS
    arriving, passed, relayed, shared = [], [], [], []
    for step in range(CHUNKS + LAG_NEG):
        for piece in work[len(work) * step // pieces : len(work) * (step + 1) // pieces]:
            piece()
        if step < CHUNKS:
            c = step
            side_pos[c].wait_recv()
            out[c].wait_recv()
            grad = pos_grad[0, span(r, c), :] + beside_pos[0, local(c), :] + far[0, local(c), :]
            fresh[local(c), :] = adagrad(0, c, grad, block[span(r, c), :])
            arriving.append(send(fresh.at[local(c), :], neg_at(1, r, c), 5, c, far_ahead))
            passed.append(send(fresh.at[local(c), :], block_next.at[span(r, c), :], 6, c, ahead))
        if 0 <= step - LAG_POS < CHUNKS:
            c = step - LAG_POS
            passed[c].wait_recv()
            shared.append(
                send(block_next.at[span(r, c), :], block_next.at[span(r, c), :], 7, c, beside)
            )
        if 0 <= step - LAG_NEG < per:
            c = step - LAG_NEG
            arriving[c].wait_recv()
            relayed.append(send(neg_at(1, r, c), neg_at(1, r, c), 8, c, beside))
    for c in range(CHUNKS):
        shared[c].wait_recv()
    prepare(1, new_users, block_next)
    out, side_pos = work_through(1, arriving, relayed, 8, far_behind)
    homeward = []
    for c in range(CHUNKS):
        side_pos[c].wait_recv()
        pos_sum[local(c), :] = pos_grad[1, span(r, c), :] + beside_pos[1, local(c), :]
        homeward.append(send(pos_sum.at[local(c), :], home_pos.at[local(c), :], 12, c, behind))
    for piece in user_work(1, new_users, True):
        piece()
    new_user_state[...] = user_sums[...].T[0:rows, :]
    last = []
    for c in range(CHUNKS):
        homeward[c].wait_recv()
        out[c].wait_recv()
        grad = home_pos[local(c), :] + far[1, local(c), :]
        new_items[span(r, c), :] = adagrad(1, c, grad, fresh[local(c), :])
        last.append(send(new_items.at[span(r, c), :], new_items.at[span(r, c), :], 13, c, beside))
    new_item_state[r] = item_sums[...].T[0 : half // side, :]
    last.append(send(new_item_state.at[r], new_item_state.at[r], 14, 0, beside))
    for copy in last:
        copy.wait_recv()
    for copy in started:
        copy.wait_send()


def run_whole(users, user_state, items, item_state, ids, positives, count, offsets):
    block, width = items.shape
    half = block // 2
    slots = ids.shape[1]
    cols = block // TILE
    tiles = users.shape[0] * cols
    arrays = (users, user_state, items, item_state, ids, positives, count, offsets)
    hbm = pltpu.MemorySpace.HBM
    square = pltpu.VMEM((TILE, TILE), f32)
    return pl.pallas_call(
        functools.partial(whole_kernel, lax.axis_size("wide")),
        out_shape=[jax.ShapeDtypeStruct(a.shape, f32) for a in arrays[:4]],
        in_specs=[pl.BlockSpec(memory_space=hbm)] * len(arrays),
        out_specs=[pl.BlockSpec(memory_space=VMEM)] * 4,
        scratch_shapes=[
            pltpu.VMEM(users.shape, f32),
            pltpu.VMEM(users.shape, bf16),
            pltpu.VMEM(users.shape, bf16),
            pltpu.VMEM(user_state.shape, f32),
            pltpu.VMEM(items.shape, f32),
            pltpu.VMEM(items.shape, f32),
            pltpu.VMEM(item_state.shape, f32),
            pltpu.VMEM(positives.shape, jnp.int32),
            pltpu.VMEM((cols, 2 * TILE, width), bf16),
            pltpu.VMEM((STRATA, GROUPS, TILE, width), f32),
            pltpu.VMEM(items.shape, bf16),
            pltpu.VMEM((slots, block, TILE), bf16),
            pltpu.VMEM((slots, TILE, width), f32),
            pltpu.VMEM((STRATA, GROUPS, TILE, width), f32),
            pltpu.VMEM((STRATA, half, width), f32),
            pltpu.VMEM((STRATA, half, width), f32),
            pltpu.VMEM((STRATA, half, width), f32),
            pltpu.VMEM((STRATA, block, width), f32),
            pltpu.VMEM((STRATA, half, width), f32),
            pltpu.VMEM((half, width), f32),
            pltpu.VMEM((half, width), f32),
            pltpu.VMEM((half, width), f32),
            pltpu.VMEM((slots + 1, TILE, width), f32),
            pltpu.VMEM((STRATA, slots, TILE, TILE), bf16),
            square, square, square, square, square,
            pltpu.VMEM((slots, 8, TILE), f32),
            pltpu.SMEM(ids.shape, jnp.int32),
            pltpu.SMEM(count.shape, jnp.int32),
            pltpu.SMEM(offsets.shape, jnp.int32),
            pltpu.SMEM((STRATA, tiles), jnp.int32),
            pltpu.SemaphoreType.DMA((2, 15, CHUNKS)),
            pltpu.SemaphoreType.DMA((len(arrays),)),
        ],
        compiler_params=pltpu.CompilerParams(
            collective_id=0, has_side_effects=True, vmem_limit_bytes=40 * 1024 * 1024
        ),
        name="whole",
    )(*[pltpu.with_memory_space_constraint(a, hbm) for a in arrays])


def passed_along(block, distance):
    size = lax.axis_size("wide")
    return lax.ppermute(block, "wide", [((i - distance) % size, i) for i in range(size)])


def general_exchange(shift, pos_grad, neg_grad, block, state):
    half = lax.axis_size("wide") // 2
    total = lax.psum(pos_grad + passed_along(neg_grad, half), "narrow")
    new_state = state + jnp.mean(total * total, axis=-1)
    block = block - step_rate * total / jnp.sqrt(new_state)[:, None]
    return passed_along((block, new_state), shift)


def per_device(users, user_state, items, item_state, tile_ids, tile_count, pos_items, neg_offsets):
    wide, narrow = lax.axis_size("wide"), lax.axis_size("narrow")
    ids, count = tile_ids[0, 0], tile_count[0]
    positives, offsets = pos_items[0, 0], neg_offsets[0, 0]
    own_state = user_state.reshape(-1, TILE)
    if narrow == 2:
        users, own_state, block, block_state = run_whole(
            users.reshape(-1, TILE, users.shape[1]), own_state, items, item_state.reshape(2, -1, TILE), ids, positives, count, offsets
        )
    else:
        block, block_state = items, item_state
        for stratum in range(STRATA):
            negatives = passed_along(block, wide // 2)
            users, own_state, pos_grad, neg_grad = run_tiles(
                stratum, ids, count, offsets, positives, users, own_state, block, negatives
            )
            shift = 1 - STRATA if stratum + 1 == STRATA else 1
            block, block_state = general_exchange(shift, pos_grad, neg_grad, block, block_state)
    return (users.reshape(-1, users.shape[-1]), own_state.reshape(user_state.shape), block, block_state.reshape(item_state.shape))


def solution(mesh):
    return jax.shard_map(
        per_device,
        mesh=mesh,
        in_specs=(
            P(("wide", "narrow"), None),
            P(("wide", "narrow")),
            P("wide", None),
            P("wide"),
            P("wide", "narrow", None, None),
            P("wide", "narrow", None),
            P("wide", "narrow", None, None, None),
            P("wide", "narrow", None, None),
        ),
        out_specs=(P(("wide", "narrow"), None), P(("wide", "narrow")), P("wide", None), P("wide")),
        check_vma=False,
    )
```

```python
import functools

import jax
import jax.numpy as jnp
from jax import lax
from jax.experimental import pallas as pl
from jax.experimental.pallas import tpu as pltpu
from jax.sharding import PartitionSpec as P

TILE = 128
STRATA = 2
BATCH = 4
GROUPS = 4
CHUNKS = 8
LAG_POS = 3
LAG_NEG = 4
WINDOW = TILE + 16
MESH = pl.DeviceIdType.MESH
step_rate = 0.25
f32 = jnp.float32
bf16 = jnp.bfloat16
VMEM = pltpu.MemorySpace.VMEM
SMEM = pltpu.MemorySpace.SMEM


def dot(a, b, dims):
    return lax.dot_general(a, b, (dims, ((), ())), preferred_element_type=f32)


def pair(x):
    high = x.astype(bf16)
    low = (x - high.astype(f32)).astype(bf16)
    return jnp.concatenate([high, low], axis=0)


def tiles_kernel(
    stratum, ids, count, offsets, positives, users, state, block, negatives,
    new_users, new_state, pos_grad, neg_grad, split, square, padded, spread,
):
    cols = block.shape[0] // TILE
    rows = users.shape[0] // TILE
    side = TILE
    width = users.shape[1]
    new_users[...] = jnp.zeros(new_users.shape, f32)
    pos_grad[...] = jnp.zeros(pos_grad.shape, f32)
    spread[...] = jnp.zeros(spread.shape, f32)
    length = negatives.shape[0]
    padded[0:length, :] = negatives[...]
    padded[length:, :] = jnp.zeros((padded.shape[0] - length, width), f32)
    for col in range(cols):
        split[col] = pair(block[col * side : (col + 1) * side, :])
    live_count = count[0, stratum]
    item = lax.broadcasted_iota(jnp.int32, (side, side), 0)
    place = lax.broadcasted_iota(jnp.int32, (side, WINDOW), 1)

    def batch(step, carry):
        work = []
        for lane in range(BATCH):
            slot = step * BATCH + lane
            tile = ids[stratum, slot]
            within = lax.rem(offsets[stratum, slot], 8)
            window = pl.ds(pl.multiple_of(offsets[stratum, slot] - within, 8), WINDOW)
            row = pl.multiple_of(lax.div(tile, cols) * side, side)
            col = lax.rem(tile, cols)
            live = jnp.where(slot < live_count, 1.0 / side, 0.0).astype(f32)
            factors = users[pl.ds(row, side), :]
            factors_low = factors.astype(bf16)
            neg_rows = padded[window, :].astype(bf16)
            hot = jnp.where(item == positives[stratum, pl.ds(slot, 1), :], 1.0, 0.0).astype(f32)
            hot_t = hot.T.astype(bf16)
            hot = hot.astype(bf16)
            pos_rows = dot(jnp.concatenate([hot_t, hot_t], axis=1), split[col], ((1,), (0,)))
            neg_score = dot(factors_low, neg_rows, ((1,), (1,)))
            pos_score = jnp.sum(factors * pos_rows, axis=-1, keepdims=True)
            chosen = jnp.logical_and(place >= within, place < within + side)
            coeffs = jnp.where(chosen, live, 0.0) / (1.0 + jnp.exp(pos_score - neg_score))
            totals = jnp.sum(coeffs, axis=-1, keepdims=True)
            coeffs_low = coeffs.astype(bf16)
            factor_grad = dot(coeffs_low, neg_rows, ((1,), (0,))) - totals * pos_rows
            positive = dot(
                jnp.concatenate([hot, hot], axis=1), pair(totals * factors), ((1,), (0,))
            )
            coeffs_t = coeffs.T.astype(bf16)
            negative = dot(
                jnp.concatenate([coeffs_t, coeffs_t], axis=1), pair(factors), ((1,), (0,))
            )
            work.append((row, col, window, factor_grad, positive, negative))
        for row, col, window, factor_grad, positive, negative in work:
            new_users[pl.ds(row, side), :] += factor_grad
            at = pl.ds(pl.multiple_of(col * side, side), side)
            pos_grad[at, :] -= positive
            spread[window, :] += negative
        return carry

    lax.fori_loop(0, lax.div(live_count + (BATCH - 1), BATCH), batch, 0)
    neg_grad[...] = spread[0:length, :]
    square[...] = jnp.zeros(square.shape, f32)
    square[0:rows, :] = state[...]
    sums = square[...].T
    for row in range(rows):
        at = slice(row * side, (row + 1) * side)
        grad = new_users[at, :]
        fresh = sums[:, row : row + 1] + jnp.sum(grad * grad, axis=-1, keepdims=True) * (1.0 / width)
        new_users[at, :] = users[at, :] - (step_rate / jnp.sqrt(fresh)) * grad
        square[:, row : row + 1] = fresh
    new_state[...] = square[...].T[0:rows, :]


def run_tiles(stratum, ids, count, offsets, positives, users, state, block, negatives):
    width = users.shape[1]
    cols = block.shape[0] // TILE
    return pl.pallas_call(
        functools.partial(tiles_kernel, stratum),
        out_shape=(
            jax.ShapeDtypeStruct(users.shape, f32),
            jax.ShapeDtypeStruct(state.shape, f32),
            jax.ShapeDtypeStruct(block.shape, f32),
            jax.ShapeDtypeStruct(block.shape, f32),
        ),
        in_specs=[pl.BlockSpec(memory_space=SMEM)] * 3 + [pl.BlockSpec(memory_space=VMEM)] * 5,
        out_specs=(pl.BlockSpec(memory_space=VMEM),) * 4,
        scratch_shapes=[
            pltpu.VMEM((cols, 2 * TILE, width), bf16),
            pltpu.VMEM((TILE, TILE), f32),
            pltpu.VMEM((block.shape[0] + 16, width), f32),
            pltpu.VMEM((block.shape[0] + 16, width), f32),
        ],
        compiler_params=pltpu.CompilerParams(vmem_limit_bytes=24 * 1024 * 1024),
        name="tiles",
    )(ids, count, offsets, positives, users, state, block, negatives)


def greet(devices):
    barrier = pltpu.get_barrier_semaphore()
    for device in devices:
        pl.semaphore_signal(barrier, inc=1, device_id=device, device_id_type=MESH)
    pl.semaphore_wait(barrier, len(devices))


def start_remote(src, dst, sems, kind, chunk, device):
    copy = pltpu.make_async_remote_copy(
        src_ref=src,
        dst_ref=dst,
        send_sem=sems.at[0, kind, chunk],
        recv_sem=sems.at[1, kind, chunk],
        device_id=device,
        device_id_type=MESH,
    )
    copy.start()
    return copy


def whole_kernel(
    wide, users_hbm, user_state_hbm, items_hbm, item_state_hbm, ids_hbm, positives_hbm, count_hbm,
    offsets_hbm,
    new_users, new_user_state, new_items, new_item_state,
    users, high, low, user_state, block, block_next, item_state, positives, split, negs, negs_low,
    coeffs, pos_rows, neg_grad, beside_neg, summed, far, pos_grad, beside_pos, pos_sum, home_pos,
    fresh, factor_grad, pos_part, hot_t, square, columns, user_sums, item_sums, scores, totals, partial,
    ids, count, offsets, slot_of, sems, local_sems,
):
    w, r = lax.axis_index("wide"), lax.axis_index("narrow")
    slots = ids.shape[1]
    rows, side, width = users.shape
    cols = block.shape[0] // side
    half = block.shape[0] // 2
    size = half // CHUNKS
    per = CHUNKS // GROUPS
    quarter = half // GROUPS

    def at(shift):
        return (lax.rem(w + shift + wide, wide), r)

    across, ahead, behind = at(wide // 2), at(1), at(-1)
    far_ahead, far_behind = at(wide // 2 + 1), at(wide // 2 - 1)
    beside = (w, 1 - r)
    greet([beside, across, ahead, behind, far_ahead, far_behind])

    def span(which, chunk):
        return pl.ds(pl.multiple_of(which * half + chunk * size, size), size)

    def inner(which, chunk):
        return pl.ds(pl.multiple_of(which * quarter + (chunk % per) * size, size), size)

    def local(chunk):
        return slice(chunk * size, (chunk + 1) * size)

    started = []

    def send(src, dst, kind, chunk, device):
        copy = start_remote(src, dst, sems, kind, chunk, device)
        started.append(copy)
        return copy

    def neg_at(stratum, which, chunk):
        return negs.at[stratum, chunk // per, inner(which, chunk), :]

    arriving = [
        send(items_hbm.at[span(r, c), :], neg_at(0, r, c), 0, c, across) for c in range(CHUNKS)
    ]
    loads = []
    for k, (src, dst) in enumerate(
        [
            (ids_hbm, ids), (count_hbm, count), (offsets_hbm, offsets), (positives_hbm, positives),
            (items_hbm, block), (users_hbm, users), (user_state_hbm, user_state),
            (item_state_hbm, item_state),
        ]
    ):
        loads.append(pltpu.make_async_copy(src, dst, local_sems.at[k]))
        loads[-1].start()
    factor_grad[slots] = jnp.zeros((side, width), f32)
    pos_part[slots] = jnp.zeros((side, width), f32)
    columns[...] = jnp.zeros(columns.shape, f32)
    square[...] = jnp.zeros(square.shape, f32)
    for load in loads:
        load.wait()

    item = lax.broadcasted_iota(jnp.int32, (side, side), 0)

    def find(tile, carry):
        for stratum in range(STRATA):
            found = jnp.int32(slots)
            for slot in range(slots):
                found = jnp.where(ids[stratum, slot] == tile, jnp.int32(slot), found)
            slot_of[stratum, tile] = found
        return carry

    lax.fori_loop(0, rows * cols, find, 0)

    def hots(stratum):
        for slot in range(slots):
            hot = jnp.where(item == positives[stratum, slot : slot + 1, :], 1.0, 0.0).astype(f32)
            hot_t[stratum, slot] = hot.T.astype(bf16)

    def split_users(source):
        def step(row, carry):
            value = source[row]
            top = value.astype(bf16)
            high[row] = top
            low[row] = (value - top.astype(f32)).astype(bf16)
            return carry

        lax.fori_loop(0, rows, step, 0)

    def row_at(stratum, slot):
        return lax.div(ids[stratum, slot], cols)

    def prepare(stratum, source, own):
        for col in range(cols):
            split[col] = pair(own[col * side : (col + 1) * side, :])

        for slot in range(slots):
            hot = hot_t[stratum, slot]
            picked = dot(
                jnp.concatenate([hot, hot], axis=1),
                split[lax.rem(ids[stratum, slot], cols)],
                ((1,), (0,)),
            )
            pos_rows[slot] = picked
            columns[:, slot : slot + 1] = jnp.sum(
                source[row_at(stratum, slot)] * picked, axis=-1, keepdims=True
            )
        scores[...] = columns[...].T
        partial[...] = jnp.zeros(partial.shape, f32)

    def group(stratum, g):
        near = negs[stratum, g].astype(bf16)
        here = slice(g * side, (g + 1) * side)
        negs_low[here, :] = near
        index = item + jnp.where(item >= quarter, half - quarter, 0) + g * quarter

        weights, tops, lows = [], [], []
        for slot in range(slots):
            top = high[row_at(stratum, slot)]
            scale = jnp.where(slot < count[0, stratum], 0.5 / side, 0.0).astype(f32)
            score = dot(near, top, ((1,), (1,)))
            place = index - offsets[stratum, slot]
            chosen = jnp.logical_and(place >= 0, place < side)
            part = jnp.where(chosen, scale, 0.0)
            part += part * jnp.tanh(0.5 * (score - scores[slot : slot + 1, :]))
            partial[slot] += jnp.sum(part.reshape(side // 8, 8, side), axis=0)
            part = part.astype(bf16)
            coeffs[slot, here, :] = part
            weights.append(part)
            tops.append(top)
            lows.append(low[row_at(stratum, slot)])
        left = jnp.concatenate(weights, axis=1)
        neg_grad[stratum, g] = dot(left, jnp.concatenate(tops, axis=0), ((1,), (0,))) + dot(
            left, jnp.concatenate(lows, axis=0), ((1,), (0,))
        )

    def add_totals():
        square[0:slots, :] = jnp.sum(partial[...], axis=1)
        totals[...] = square[...].T

    def positive_part(stratum, slot):
        chosen = item == positives[stratum, slot : slot + 1, :]
        hot = jnp.where(chosen, square[slot : slot + 1, :], 0.0)
        top = hot.astype(bf16)
        rest = (hot - top.astype(f32)).astype(bf16)
        upper, lower = high[row_at(stratum, slot)], low[row_at(stratum, slot)]
        pos_part[slot] = dot(
            jnp.concatenate([top, rest], axis=1),
            jnp.concatenate([upper, upper], axis=0),
            ((1,), (0,)),
        ) + dot(top, lower, ((1,), (0,)))

    def positive(stratum, which):
        for k in range(cols // 2):
            col = which * (cols // 2) + k
            total = pos_part[slot_of[stratum, col]]
            for row in range(1, rows):
                total += pos_part[slot_of[stratum, row * cols + col]]
            pos_grad[stratum, pl.ds(pl.multiple_of(col * side, side), side), :] = -total

    def factor_part(slot):
        factor_grad[slot] = (
            dot(coeffs[slot], negs_low[...], ((0,), (0,)))
            - totals[:, slot : slot + 1] * pos_rows[slot]
        )

    def update_part(stratum, row, source, last):
        grad = factor_grad[slot_of[stratum, row * cols]]
        for col in range(1, cols):
            grad += factor_grad[slot_of[stratum, row * cols + col]]
        sums = user_sums[:, row : row + 1] + jnp.sum(grad * grad, axis=-1, keepdims=True) * (
            1.0 / width
        )
        value = source[row] - (step_rate / jnp.sqrt(sums)) * grad
        user_sums[:, row : row + 1] = sums
        new_users[row] = value
        if not last:
            top = value.astype(bf16)
            high[row] = top
            low[row] = (value - top.astype(f32)).astype(bf16)

    def user_work(stratum, source, last):
        for slot in range(slots):
            yield functools.partial(factor_part, slot)
        for row in range(rows):
            yield functools.partial(update_part, stratum, row, source, last)

    def adagrad(stratum, c, grad, value):
        col, begin = c * size // side, c * size % side
        sums = item_sums[begin : begin + size, col : col + 1] + jnp.sum(
            grad * grad, axis=-1, keepdims=True
        ) * (1.0 / width)
        item_sums[begin : begin + size, col : col + 1] = sums
        return value - (step_rate / jnp.sqrt(sums)) * grad

    square[0:rows, :] = user_state[...]
    user_sums[...] = square[...].T
    square[0 : half // side, :] = item_state[r]
    item_sums[...] = square[...].T
    for stratum in range(STRATA):
        hots(stratum)
    split_users(users)
    prepare(0, users, block)

    def chunks_of(g):
        return range(g * per, (g + 1) * per)

    def work_through(stratum, arriving, relayed, kind, target):
        side_neg, out = [], []

        def relay(c):
            arriving[c].wait_recv()
            relayed.append(send(neg_at(stratum, r, c), neg_at(stratum, r, c), kind, c, beside))

        def add(g):
            for c in chunks_of(g):
                side_neg[c].wait_recv()
                summed[stratum, local(c), :] = (
                    neg_grad[stratum, g, inner(r, c), :] + beside_neg[stratum, local(c), :]
                )
                out.append(
                    send(
                        summed.at[stratum, local(c), :], far.at[stratum, local(c), :],
                        kind + 2, c, target,
                    )
                )

        for g in range(GROUPS):
            for c in range(len(relayed), (g + 1) * per):
                relay(c)
            for c in chunks_of(g):
                relayed[c].wait_recv()
            if g + 1 < GROUPS:
                for c in range(len(relayed), (g + 2) * per):
                    relay(c)
            group(stratum, g)
            for c in chunks_of(g):
                side_neg.append(
                    send(
                        neg_grad.at[stratum, g, inner(1 - r, c), :],
                        beside_neg.at[stratum, local(c), :],
                        kind + 1, c, beside,
                    )
                )
            if g > 0:
                add(g - 1)
        add_totals()
        for slot in range(slots):
            positive_part(stratum, slot)
        positive(stratum, 1 - r)
        side_pos = [
            send(
                pos_grad.at[stratum, span(1 - r, c), :], beside_pos.at[stratum, local(c), :],
                kind + 3, c, beside,
            )
            for c in range(CHUNKS)
        ]
        add(GROUPS - 1)
        positive(stratum, r)
        return out, side_pos

    out, side_pos = work_through(0, arriving, [], 1, across)
    work = list(user_work(0, users, False))
    pieces = CHUNKS + LAG_POS
    arriving, passed, relayed, shared = [], [], [], []
    for step in range(CHUNKS + LAG_NEG):
        for piece in work[len(work) * step // pieces : len(work) * (step + 1) // pieces]:
            piece()
        if step < CHUNKS:
            c = step
            side_pos[c].wait_recv()
            out[c].wait_recv()
            grad = pos_grad[0, span(r, c), :] + beside_pos[0, local(c), :] + far[0, local(c), :]
            fresh[local(c), :] = adagrad(0, c, grad, block[span(r, c), :])
            arriving.append(send(fresh.at[local(c), :], neg_at(1, r, c), 5, c, far_ahead))
            passed.append(send(fresh.at[local(c), :], block_next.at[span(r, c), :], 6, c, ahead))
        if 0 <= step - LAG_POS < CHUNKS:
            c = step - LAG_POS
            passed[c].wait_recv()
            shared.append(
                send(block_next.at[span(r, c), :], block_next.at[span(r, c), :], 7, c, beside)
            )
        if 0 <= step - LAG_NEG < per:
            c = step - LAG_NEG
            arriving[c].wait_recv()
            relayed.append(send(neg_at(1, r, c), neg_at(1, r, c), 8, c, beside))
    for c in range(CHUNKS):
        shared[c].wait_recv()
    prepare(1, new_users, block_next)
    out, side_pos = work_through(1, arriving, relayed, 8, far_behind)
    homeward = []
    for c in range(CHUNKS):
        side_pos[c].wait_recv()
        pos_sum[local(c), :] = pos_grad[1, span(r, c), :] + beside_pos[1, local(c), :]
        homeward.append(send(pos_sum.at[local(c), :], home_pos.at[local(c), :], 12, c, behind))
    for piece in user_work(1, new_users, True):
        piece()
    new_user_state[...] = user_sums[...].T[0:rows, :]
    last = []
    for c in range(CHUNKS):
        homeward[c].wait_recv()
        out[c].wait_recv()
        grad = home_pos[local(c), :] + far[1, local(c), :]
        new_items[span(r, c), :] = adagrad(1, c, grad, fresh[local(c), :])
        last.append(send(new_items.at[span(r, c), :], new_items.at[span(r, c), :], 13, c, beside))
    new_item_state[r] = item_sums[...].T[0 : half // side, :]
    last.append(send(new_item_state.at[r], new_item_state.at[r], 14, 0, beside))
    for copy in last:
        copy.wait_recv()
    for copy in started:
        copy.wait_send()


def run_whole(users, user_state, items, item_state, ids, positives, count, offsets):
    block, width = items.shape
    half = block // 2
    slots = ids.shape[1]
    cols = block // TILE
    tiles = users.shape[0] * cols
    arrays = (users, user_state, items, item_state, ids, positives, count, offsets)
    hbm = pltpu.MemorySpace.HBM
    square = pltpu.VMEM((TILE, TILE), f32)
    return pl.pallas_call(
        functools.partial(whole_kernel, lax.axis_size("wide")),
        out_shape=[jax.ShapeDtypeStruct(a.shape, f32) for a in arrays[:4]],
        in_specs=[pl.BlockSpec(memory_space=hbm)] * len(arrays),
        out_specs=[pl.BlockSpec(memory_space=VMEM)] * 4,
        scratch_shapes=[
            pltpu.VMEM(users.shape, f32),
            pltpu.VMEM(users.shape, bf16),
            pltpu.VMEM(users.shape, bf16),
            pltpu.VMEM(user_state.shape, f32),
            pltpu.VMEM(items.shape, f32),
            pltpu.VMEM(items.shape, f32),
            pltpu.VMEM(item_state.shape, f32),
            pltpu.VMEM(positives.shape, jnp.int32),
            pltpu.VMEM((cols, 2 * TILE, width), bf16),
            pltpu.VMEM((STRATA, GROUPS, TILE, width), f32),
            pltpu.VMEM(items.shape, bf16),
            pltpu.VMEM((slots, block, TILE), bf16),
            pltpu.VMEM((slots, TILE, width), f32),
            pltpu.VMEM((STRATA, GROUPS, TILE, width), f32),
            pltpu.VMEM((STRATA, half, width), f32),
            pltpu.VMEM((STRATA, half, width), f32),
            pltpu.VMEM((STRATA, half, width), f32),
            pltpu.VMEM((STRATA, block, width), f32),
            pltpu.VMEM((STRATA, half, width), f32),
            pltpu.VMEM((half, width), f32),
            pltpu.VMEM((half, width), f32),
            pltpu.VMEM((half, width), f32),
            pltpu.VMEM((slots + 1, TILE, width), f32),
            pltpu.VMEM((slots + 1, TILE, width), f32),
            pltpu.VMEM((STRATA, slots, TILE, TILE), bf16),
            square, square, square, square, square, square,
            pltpu.VMEM((slots, 8, TILE), f32),
            pltpu.SMEM(ids.shape, jnp.int32),
            pltpu.SMEM(count.shape, jnp.int32),
            pltpu.SMEM(offsets.shape, jnp.int32),
            pltpu.SMEM((STRATA, tiles), jnp.int32),
            pltpu.SemaphoreType.DMA((2, 15, CHUNKS)),
            pltpu.SemaphoreType.DMA((len(arrays),)),
        ],
        compiler_params=pltpu.CompilerParams(
            collective_id=0, has_side_effects=True, vmem_limit_bytes=40 * 1024 * 1024
        ),
        name="whole",
    )(*[pltpu.with_memory_space_constraint(a, hbm) for a in arrays])


def passed_along(block, distance):
    size = lax.axis_size("wide")
    return lax.ppermute(block, "wide", [((i - distance) % size, i) for i in range(size)])


def general_exchange(shift, pos_grad, neg_grad, block, state):
    half = lax.axis_size("wide") // 2
    total = lax.psum(pos_grad + passed_along(neg_grad, half), "narrow")
    new_state = state + jnp.mean(total * total, axis=-1)
    block = block - step_rate * total / jnp.sqrt(new_state)[:, None]
    return passed_along((block, new_state), shift)


def per_device(users, user_state, items, item_state, tile_ids, tile_count, pos_items, neg_offsets):
    wide, narrow = lax.axis_size("wide"), lax.axis_size("narrow")
    ids, count = tile_ids[0, 0], tile_count[0]
    positives, offsets = pos_items[0, 0], neg_offsets[0, 0]
    own_state = user_state.reshape(-1, TILE)
    if narrow == 2:
        users, own_state, block, block_state = run_whole(
            users.reshape(-1, TILE, users.shape[1]), own_state, items, item_state.reshape(2, -1, TILE), ids, positives, count, offsets
        )
    else:
        block, block_state = items, item_state
        for stratum in range(STRATA):
            negatives = passed_along(block, wide // 2)
            users, own_state, pos_grad, neg_grad = run_tiles(
                stratum, ids, count, offsets, positives, users, own_state, block, negatives
            )
            shift = 1 - STRATA if stratum + 1 == STRATA else 1
            block, block_state = general_exchange(shift, pos_grad, neg_grad, block, block_state)
    return (users.reshape(-1, users.shape[-1]), own_state.reshape(user_state.shape), block, block_state.reshape(item_state.shape))


def solution(mesh):
    return jax.shard_map(
        per_device,
        mesh=mesh,
        in_specs=(
            P(("wide", "narrow"), None),
            P(("wide", "narrow")),
            P("wide", None),
            P("wide"),
            P("wide", "narrow", None, None),
            P("wide", "narrow", None),
            P("wide", "narrow", None, None, None),
            P("wide", "narrow", None, None),
        ),
        out_specs=(P(("wide", "narrow"), None), P(("wide", "narrow")), P("wide", None), P("wide")),
        check_vma=False,
    )
```

```python
import functools

import jax
import jax.numpy as jnp
from jax import lax
from jax.experimental import pallas as pl
from jax.experimental.pallas import tpu as pltpu
from jax.sharding import PartitionSpec as P

TILE = 128
STRATA = 2
BATCH = 4
GROUPS = 4
CHUNKS = 8
LAG_POS = 3
LAG_NEG = 4
WINDOW = TILE + 16
MESH = pl.DeviceIdType.MESH
step_rate = 0.25
f32 = jnp.float32
bf16 = jnp.bfloat16
VMEM = pltpu.MemorySpace.VMEM
SMEM = pltpu.MemorySpace.SMEM


def dot(a, b, dims):
    return lax.dot_general(a, b, (dims, ((), ())), preferred_element_type=f32)


def pair(x):
    high = x.astype(bf16)
    low = (x - high.astype(f32)).astype(bf16)
    return jnp.concatenate([high, low], axis=0)


def tiles_kernel(
    stratum, ids, count, offsets, positives, users, state, block, negatives,
    new_users, new_state, pos_grad, neg_grad, split, square, padded, spread,
):
    cols = block.shape[0] // TILE
    rows = users.shape[0] // TILE
    side = TILE
    width = users.shape[1]
    new_users[...] = jnp.zeros(new_users.shape, f32)
    pos_grad[...] = jnp.zeros(pos_grad.shape, f32)
    spread[...] = jnp.zeros(spread.shape, f32)
    length = negatives.shape[0]
    padded[0:length, :] = negatives[...]
    padded[length:, :] = jnp.zeros((padded.shape[0] - length, width), f32)
    for col in range(cols):
        split[col] = pair(block[col * side : (col + 1) * side, :])
    live_count = count[0, stratum]
    item = lax.broadcasted_iota(jnp.int32, (side, side), 0)
    place = lax.broadcasted_iota(jnp.int32, (side, WINDOW), 1)

    def batch(step, carry):
        work = []
        for lane in range(BATCH):
            slot = step * BATCH + lane
            tile = ids[stratum, slot]
            within = lax.rem(offsets[stratum, slot], 8)
            window = pl.ds(pl.multiple_of(offsets[stratum, slot] - within, 8), WINDOW)
            row = pl.multiple_of(lax.div(tile, cols) * side, side)
            col = lax.rem(tile, cols)
            live = jnp.where(slot < live_count, 1.0 / side, 0.0).astype(f32)
            factors = users[pl.ds(row, side), :]
            factors_low = factors.astype(bf16)
            neg_rows = padded[window, :].astype(bf16)
            hot = jnp.where(item == positives[stratum, pl.ds(slot, 1), :], 1.0, 0.0).astype(f32)
            hot_t = hot.T.astype(bf16)
            hot = hot.astype(bf16)
            pos_rows = dot(jnp.concatenate([hot_t, hot_t], axis=1), split[col], ((1,), (0,)))
            neg_score = dot(factors_low, neg_rows, ((1,), (1,)))
            pos_score = jnp.sum(factors * pos_rows, axis=-1, keepdims=True)
            chosen = jnp.logical_and(place >= within, place < within + side)
            coeffs = jnp.where(chosen, live, 0.0) / (1.0 + jnp.exp(pos_score - neg_score))
            totals = jnp.sum(coeffs, axis=-1, keepdims=True)
            coeffs_low = coeffs.astype(bf16)
            factor_grad = dot(coeffs_low, neg_rows, ((1,), (0,))) - totals * pos_rows
            positive = dot(
                jnp.concatenate([hot, hot], axis=1), pair(totals * factors), ((1,), (0,))
            )
            coeffs_t = coeffs.T.astype(bf16)
            negative = dot(
                jnp.concatenate([coeffs_t, coeffs_t], axis=1), pair(factors), ((1,), (0,))
            )
            work.append((row, col, window, factor_grad, positive, negative))
        for row, col, window, factor_grad, positive, negative in work:
            new_users[pl.ds(row, side), :] += factor_grad
            at = pl.ds(pl.multiple_of(col * side, side), side)
            pos_grad[at, :] -= positive
            spread[window, :] += negative
        return carry

    lax.fori_loop(0, lax.div(live_count + (BATCH - 1), BATCH), batch, 0)
    neg_grad[...] = spread[0:length, :]
    square[...] = jnp.zeros(square.shape, f32)
    square[0:rows, :] = state[...]
    sums = square[...].T
    for row in range(rows):
        at = slice(row * side, (row + 1) * side)
        grad = new_users[at, :]
        fresh = sums[:, row : row + 1] + jnp.sum(grad * grad, axis=-1, keepdims=True) * (1.0 / width)
        new_users[at, :] = users[at, :] - (step_rate / jnp.sqrt(fresh)) * grad
        square[:, row : row + 1] = fresh
    new_state[...] = square[...].T[0:rows, :]


def run_tiles(stratum, ids, count, offsets, positives, users, state, block, negatives):
    width = users.shape[1]
    cols = block.shape[0] // TILE
    return pl.pallas_call(
        functools.partial(tiles_kernel, stratum),
        out_shape=(
            jax.ShapeDtypeStruct(users.shape, f32),
            jax.ShapeDtypeStruct(state.shape, f32),
            jax.ShapeDtypeStruct(block.shape, f32),
            jax.ShapeDtypeStruct(block.shape, f32),
        ),
        in_specs=[pl.BlockSpec(memory_space=SMEM)] * 3 + [pl.BlockSpec(memory_space=VMEM)] * 5,
        out_specs=(pl.BlockSpec(memory_space=VMEM),) * 4,
        scratch_shapes=[
            pltpu.VMEM((cols, 2 * TILE, width), bf16),
            pltpu.VMEM((TILE, TILE), f32),
            pltpu.VMEM((block.shape[0] + 16, width), f32),
            pltpu.VMEM((block.shape[0] + 16, width), f32),
        ],
        compiler_params=pltpu.CompilerParams(vmem_limit_bytes=24 * 1024 * 1024),
        name="tiles",
    )(ids, count, offsets, positives, users, state, block, negatives)


def greet(devices):
    barrier = pltpu.get_barrier_semaphore()
    for device in devices:
        pl.semaphore_signal(barrier, inc=1, device_id=device, device_id_type=MESH)
    pl.semaphore_wait(barrier, len(devices))


def start_remote(src, dst, sems, kind, chunk, device):
    copy = pltpu.make_async_remote_copy(
        src_ref=src,
        dst_ref=dst,
        send_sem=sems.at[0, kind, chunk],
        recv_sem=sems.at[1, kind, chunk],
        device_id=device,
        device_id_type=MESH,
    )
    copy.start()
    return copy


def whole_kernel(
    wide, users_hbm, user_state_hbm, items_hbm, item_state_hbm, ids_hbm, positives_hbm, count_hbm,
    offsets_hbm,
    new_users, new_user_state, new_items, new_item_state,
    users, high, low, user_state, block, block_next, item_state, positives, split, negs, negs_low,
    coeffs, pos_rows, neg_grad, beside_neg, summed, far, pos_grad, beside_pos, pos_sum, home_pos,
    fresh, factor_grad, pos_part, hot_t, square, columns, user_sums, item_sums, scores, totals, partial,
    ids, count, offsets, slot_of, sems, local_sems,
):
    w, r = lax.axis_index("wide"), lax.axis_index("narrow")
    slots = ids.shape[1]
    rows, side, width = users.shape
    cols = block.shape[0] // side
    half = block.shape[0] // 2
    size = half // CHUNKS
    per = CHUNKS // GROUPS
    quarter = half // GROUPS

    def at(shift):
        return (lax.rem(w + shift + wide, wide), r)

    across, ahead, behind = at(wide // 2), at(1), at(-1)
    far_ahead, far_behind = at(wide // 2 + 1), at(wide // 2 - 1)
    beside = (w, 1 - r)
    greet([beside, across, ahead, behind, far_ahead, far_behind])

    def span(which, chunk):
        return pl.ds(pl.multiple_of(which * half + chunk * size, size), size)

    def inner(which, chunk):
        return pl.ds(pl.multiple_of(which * quarter + (chunk % per) * size, size), size)

    def local(chunk):
        return slice(chunk * size, (chunk + 1) * size)

    started = []

    def send(src, dst, kind, chunk, device):
        copy = start_remote(src, dst, sems, kind, chunk, device)
        started.append(copy)
        return copy

    def neg_at(stratum, which, chunk):
        return negs.at[stratum, chunk // per, inner(which, chunk), :]

    arriving = [
        send(items_hbm.at[span(r, c), :], neg_at(0, r, c), 0, c, across) for c in range(CHUNKS)
    ]
    loads = []
    for k, (src, dst) in enumerate(
        [
            (ids_hbm, ids), (count_hbm, count), (offsets_hbm, offsets), (positives_hbm, positives),
            (items_hbm, block), (users_hbm, users), (user_state_hbm, user_state),
            (item_state_hbm, item_state),
        ]
    ):
        loads.append(pltpu.make_async_copy(src, dst, local_sems.at[k]))
        loads[-1].start()
    factor_grad[slots] = jnp.zeros((side, width), f32)
    pos_part[slots] = jnp.zeros((side, width), f32)
    columns[...] = jnp.zeros(columns.shape, f32)
    square[...] = jnp.zeros(square.shape, f32)
    for load in loads:
        load.wait()

    item = lax.broadcasted_iota(jnp.int32, (side, side), 0)

    def find(tile, carry):
        for stratum in range(STRATA):
            found = jnp.int32(slots)
            for slot in range(slots):
                found = jnp.where(ids[stratum, slot] == tile, jnp.int32(slot), found)
            slot_of[stratum, tile] = found
        return carry

    def hots(stratum):
        for slot in range(slots):
            hot = jnp.where(item == positives[stratum, slot : slot + 1, :], 1.0, 0.0).astype(f32)
            hot_t[stratum, slot] = hot.T.astype(bf16)

    def split_users(source):
        def step(row, carry):
            value = source[row]
            top = value.astype(bf16)
            high[row] = top
            low[row] = (value - top.astype(f32)).astype(bf16)
            return carry

        lax.fori_loop(0, rows, step, 0)

    def row_at(stratum, slot):
        return lax.div(ids[stratum, slot], cols)

    def prepare(stratum, source, own):
        for col in range(cols):
            split[col] = pair(own[col * side : (col + 1) * side, :])

        for slot in range(slots):
            hot = hot_t[stratum, slot]
            picked = dot(
                jnp.concatenate([hot, hot], axis=1),
                split[lax.rem(ids[stratum, slot], cols)],
                ((1,), (0,)),
            )
            pos_rows[slot] = picked
            columns[:, slot : slot + 1] = jnp.sum(
                source[row_at(stratum, slot)] * picked, axis=-1, keepdims=True
            )
        scores[...] = columns[...].T
        partial[...] = jnp.zeros(partial.shape, f32)

    def group(stratum, g):
        near = negs[stratum, g].astype(bf16)
        here = slice(g * side, (g + 1) * side)
        negs_low[here, :] = near
        index = item + jnp.where(item >= quarter, half - quarter, 0) + g * quarter

        weights, tops, lows = [], [], []
        for slot in range(slots):
            top = high[row_at(stratum, slot)]
            scale = jnp.where(slot < count[0, stratum], 0.5 / side, 0.0).astype(f32)
            score = dot(near, top, ((1,), (1,)))
            place = index - offsets[stratum, slot]
            chosen = jnp.logical_and(place >= 0, place < side)
            part = jnp.where(chosen, scale, 0.0)
            part += part * jnp.tanh(0.5 * (score - scores[slot : slot + 1, :]))
            partial[slot] += jnp.sum(part.reshape(side // 8, 8, side), axis=0)
            part = part.astype(bf16)
            coeffs[slot, here, :] = part
            weights.append(part)
            tops.append(top)
            lows.append(low[row_at(stratum, slot)])
        left = jnp.concatenate(weights, axis=1)
        neg_grad[stratum, g] = dot(left, jnp.concatenate(tops, axis=0), ((1,), (0,))) + dot(
            left, jnp.concatenate(lows, axis=0), ((1,), (0,))
        )

    def add_totals():
        square[0:slots, :] = jnp.sum(partial[...], axis=1)
        totals[...] = square[...].T

    def positive_part(stratum, slot):
        chosen = item == positives[stratum, slot : slot + 1, :]
        hot = jnp.where(chosen, square[slot : slot + 1, :], 0.0)
        top = hot.astype(bf16)
        rest = (hot - top.astype(f32)).astype(bf16)
        upper, lower = high[row_at(stratum, slot)], low[row_at(stratum, slot)]
        pos_part[slot] = dot(
            jnp.concatenate([top, rest], axis=1),
            jnp.concatenate([upper, upper], axis=0),
            ((1,), (0,)),
        ) + dot(top, lower, ((1,), (0,)))

    def positive(stratum, which):
        for k in range(cols // 2):
            col = which * (cols // 2) + k
            total = pos_part[slot_of[stratum, col]]
            for row in range(1, rows):
                total += pos_part[slot_of[stratum, row * cols + col]]
            pos_grad[stratum, pl.ds(pl.multiple_of(col * side, side), side), :] = -total

    def factor_part(slot):
        factor_grad[slot] = (
            dot(coeffs[slot], negs_low[...], ((0,), (0,)))
            - totals[:, slot : slot + 1] * pos_rows[slot]
        )

    def update_part(stratum, row, source, last):
        grad = factor_grad[slot_of[stratum, row * cols]]
        for col in range(1, cols):
            grad += factor_grad[slot_of[stratum, row * cols + col]]
        sums = user_sums[:, row : row + 1] + jnp.sum(grad * grad, axis=-1, keepdims=True) * (
            1.0 / width
        )
        value = source[row] - (step_rate / jnp.sqrt(sums)) * grad
        user_sums[:, row : row + 1] = sums
        new_users[row] = value
        if not last:
            top = value.astype(bf16)
            high[row] = top
            low[row] = (value - top.astype(f32)).astype(bf16)

    def user_work(stratum, source, last):
        for slot in range(slots):
            yield functools.partial(factor_part, slot)
        for row in range(rows):
            yield functools.partial(update_part, stratum, row, source, last)

    def adagrad(stratum, c, grad, value):
        col, begin = c * size // side, c * size % side
        sums = item_sums[begin : begin + size, col : col + 1] + jnp.sum(
            grad * grad, axis=-1, keepdims=True
        ) * (1.0 / width)
        item_sums[begin : begin + size, col : col + 1] = sums
        return value - (step_rate / jnp.sqrt(sums)) * grad

    square[0:rows, :] = user_state[...]
    user_sums[...] = square[...].T
    square[0 : half // side, :] = item_state[r]
    item_sums[...] = square[...].T
    hots(0)
    split_users(users)
    prepare(0, users, block)

    def chunks_of(g):
        return range(g * per, (g + 1) * per)

    def work_through(stratum, arriving, relayed, kind, target, filler):
        side_neg, out = [], []

        def relay(c):
            arriving[c].wait_recv()
            relayed.append(send(neg_at(stratum, r, c), neg_at(stratum, r, c), kind, c, beside))

        def add(g):
            for c in chunks_of(g):
                side_neg[c].wait_recv()
                summed[stratum, local(c), :] = (
                    neg_grad[stratum, g, inner(r, c), :] + beside_neg[stratum, local(c), :]
                )
                out.append(
                    send(
                        summed.at[stratum, local(c), :], far.at[stratum, local(c), :],
                        kind + 2, c, target,
                    )
                )

        for g in range(GROUPS):
            for c in range(len(relayed), (g + 1) * per):
                relay(c)
            for c in chunks_of(g):
                relayed[c].wait_recv()
            if g + 1 < GROUPS:
                for c in range(len(relayed), (g + 2) * per):
                    relay(c)
            if g == GROUPS - 2:
                for before in range(g - 1):
                    add(before)
            group(stratum, g)
            for c in chunks_of(g):
                side_neg.append(
                    send(
                        neg_grad.at[stratum, g, inner(1 - r, c), :],
                        beside_neg.at[stratum, local(c), :],
                        kind + 1, c, beside,
                    )
                )
            if g == 0:
                filler()
            if g >= GROUPS - 2:
                add(g - 1)
        add_totals()
        for slot in range(slots):
            positive_part(stratum, slot)
        positive(stratum, 1 - r)
        side_pos = [
            send(
                pos_grad.at[stratum, span(1 - r, c), :], beside_pos.at[stratum, local(c), :],
                kind + 3, c, beside,
            )
            for c in range(CHUNKS)
        ]
        add(GROUPS - 1)
        positive(stratum, r)
        return out, side_pos

    def prepare_later():
        lax.fori_loop(0, rows * cols, find, 0)
        hots(1)

    out, side_pos = work_through(0, arriving, [], 1, across, prepare_later)
    work = list(user_work(0, users, False))
    pieces = CHUNKS + LAG_POS
    arriving, passed, relayed, shared = [], [], [], []
    for step in range(CHUNKS + LAG_NEG):
        for piece in work[len(work) * step // pieces : len(work) * (step + 1) // pieces]:
            piece()
        if step < CHUNKS:
            c = step
            side_pos[c].wait_recv()
            out[c].wait_recv()
            grad = pos_grad[0, span(r, c), :] + beside_pos[0, local(c), :] + far[0, local(c), :]
            fresh[local(c), :] = adagrad(0, c, grad, block[span(r, c), :])
            arriving.append(send(fresh.at[local(c), :], neg_at(1, r, c), 5, c, far_ahead))
            passed.append(send(fresh.at[local(c), :], block_next.at[span(r, c), :], 6, c, ahead))
        if 0 <= step - LAG_POS < CHUNKS:
            c = step - LAG_POS
            passed[c].wait_recv()
            shared.append(
                send(block_next.at[span(r, c), :], block_next.at[span(r, c), :], 7, c, beside)
            )
        if 0 <= step - LAG_NEG < 2 * per:
            c = step - LAG_NEG
            arriving[c].wait_recv()
            relayed.append(send(neg_at(1, r, c), neg_at(1, r, c), 8, c, beside))
    for c in range(CHUNKS):
        shared[c].wait_recv()
    prepare(1, new_users, block_next)
    out, side_pos = work_through(1, arriving, relayed, 8, far_behind, lambda: None)
    homeward, last = [], []
    work = list(user_work(1, new_users, True))
    steps = 2 * CHUNKS
    for step in range(steps):
        for piece in work[len(work) * step // steps : len(work) * (step + 1) // steps]:
            piece()
        c = step % CHUNKS
        if step < CHUNKS:
            side_pos[c].wait_recv()
            pos_sum[local(c), :] = pos_grad[1, span(r, c), :] + beside_pos[1, local(c), :]
            homeward.append(send(pos_sum.at[local(c), :], home_pos.at[local(c), :], 12, c, behind))
        else:
            homeward[c].wait_recv()
            out[c].wait_recv()
            grad = home_pos[local(c), :] + far[1, local(c), :]
            new_items[span(r, c), :] = adagrad(1, c, grad, fresh[local(c), :])
            here = new_items.at[span(r, c), :]
            last.append(send(here, here, 13, c, beside))
    new_user_state[...] = user_sums[...].T[0:rows, :]
    new_item_state[r] = item_sums[...].T[0 : half // side, :]
    last.append(send(new_item_state.at[r], new_item_state.at[r], 14, 0, beside))
    for copy in last:
        copy.wait_recv()
    for copy in started:
        copy.wait_send()


def run_whole(users, user_state, items, item_state, ids, positives, count, offsets):
    block, width = items.shape
    half = block // 2
    slots = ids.shape[1]
    cols = block // TILE
    tiles = users.shape[0] * cols
    arrays = (users, user_state, items, item_state, ids, positives, count, offsets)
    hbm = pltpu.MemorySpace.HBM
    square = pltpu.VMEM((TILE, TILE), f32)
    results = pl.pallas_call(
        functools.partial(whole_kernel, lax.axis_size("wide")),
        out_shape=[jax.ShapeDtypeStruct(a.shape, f32) for a in arrays[:4]],
        in_specs=[pl.BlockSpec(memory_space=hbm)] * len(arrays),
        out_specs=[pl.BlockSpec(memory_space=VMEM)] * 4,
        scratch_shapes=[
            pltpu.VMEM(users.shape, f32),
            pltpu.VMEM(users.shape, bf16),
            pltpu.VMEM(users.shape, bf16),
            pltpu.VMEM(user_state.shape, f32),
            pltpu.VMEM(items.shape, f32),
            pltpu.VMEM(items.shape, f32),
            pltpu.VMEM(item_state.shape, f32),
            pltpu.VMEM(positives.shape, jnp.int32),
            pltpu.VMEM((cols, 2 * TILE, width), bf16),
            pltpu.VMEM((STRATA, GROUPS, TILE, width), f32),
            pltpu.VMEM(items.shape, bf16),
            pltpu.VMEM((slots, block, TILE), bf16),
            pltpu.VMEM((slots, TILE, width), f32),
            pltpu.VMEM((STRATA, GROUPS, TILE, width), f32),
            pltpu.VMEM((STRATA, half, width), f32),
            pltpu.VMEM((STRATA, half, width), f32),
            pltpu.VMEM((STRATA, half, width), f32),
            pltpu.VMEM((STRATA, block, width), f32),
            pltpu.VMEM((STRATA, half, width), f32),
            pltpu.VMEM((half, width), f32),
            pltpu.VMEM((half, width), f32),
            pltpu.VMEM((half, width), f32),
            pltpu.VMEM((slots + 1, TILE, width), f32),
            pltpu.VMEM((slots + 1, TILE, width), f32),
            pltpu.VMEM((STRATA, slots, TILE, TILE), bf16),
            square, square, square, square, square, square,
            pltpu.VMEM((slots, 8, TILE), f32),
            pltpu.SMEM(ids.shape, jnp.int32),
            pltpu.SMEM(count.shape, jnp.int32),
            pltpu.SMEM(offsets.shape, jnp.int32),
            pltpu.SMEM((STRATA, tiles), jnp.int32),
            pltpu.SemaphoreType.DMA((2, 15, CHUNKS)),
            pltpu.SemaphoreType.DMA((len(arrays),)),
        ],
        compiler_params=pltpu.CompilerParams(
            collective_id=0, has_side_effects=True, vmem_limit_bytes=40 * 1024 * 1024
        ),
        name="whole",
    )(*[pltpu.with_memory_space_constraint(a, hbm) for a in arrays])
    return write_results(results)


def results_kernel(count, *refs):
    sems = refs[-1]
    copies = [
        pltpu.make_async_copy(refs[k], refs[count + k], sems.at[k]) for k in range(count)
    ]
    for copy in copies:
        copy.start()
    for copy in copies:
        copy.wait()


def write_results(arrays):
    count = len(arrays)
    return pl.pallas_call(
        functools.partial(results_kernel, count),
        out_shape=[jax.ShapeDtypeStruct(a.shape, a.dtype) for a in arrays],
        in_specs=[pl.BlockSpec(memory_space=VMEM)] * count,
        out_specs=[pl.BlockSpec(memory_space=pltpu.MemorySpace.HBM)] * count,
        scratch_shapes=[pltpu.SemaphoreType.DMA((count,))],
        compiler_params=pltpu.CompilerParams(vmem_limit_bytes=1024 * 1024),
        name="results",
    )(*arrays)


def passed_along(block, distance):
    size = lax.axis_size("wide")
    return lax.ppermute(block, "wide", [((i - distance) % size, i) for i in range(size)])


def general_exchange(shift, pos_grad, neg_grad, block, state):
    half = lax.axis_size("wide") // 2
    total = lax.psum(pos_grad + passed_along(neg_grad, half), "narrow")
    new_state = state + jnp.mean(total * total, axis=-1)
    block = block - step_rate * total / jnp.sqrt(new_state)[:, None]
    return passed_along((block, new_state), shift)


def per_device(users, user_state, items, item_state, tile_ids, tile_count, pos_items, neg_offsets):
    wide, narrow = lax.axis_size("wide"), lax.axis_size("narrow")
    ids, count = tile_ids[0, 0], tile_count[0]
    positives, offsets = pos_items[0, 0], neg_offsets[0, 0]
    own_state = user_state.reshape(-1, TILE)
    if narrow == 2:
        users, own_state, block, block_state = run_whole(
            users.reshape(-1, TILE, users.shape[1]), own_state, items, item_state.reshape(2, -1, TILE), ids, positives, count, offsets
        )
    else:
        block, block_state = items, item_state
        for stratum in range(STRATA):
            negatives = passed_along(block, wide // 2)
            users, own_state, pos_grad, neg_grad = run_tiles(
                stratum, ids, count, offsets, positives, users, own_state, block, negatives
            )
            shift = 1 - STRATA if stratum + 1 == STRATA else 1
            block, block_state = general_exchange(shift, pos_grad, neg_grad, block, block_state)
    return (users.reshape(-1, users.shape[-1]), own_state.reshape(user_state.shape), block, block_state.reshape(item_state.shape))


def solution(mesh):
    return jax.shard_map(
        per_device,
        mesh=mesh,
        in_specs=(
            P(("wide", "narrow"), None),
            P(("wide", "narrow")),
            P("wide", None),
            P("wide"),
            P("wide", "narrow", None, None),
            P("wide", "narrow", None),
            P("wide", "narrow", None, None, None),
            P("wide", "narrow", None, None),
        ),
        out_specs=(P(("wide", "narrow"), None), P(("wide", "narrow")), P("wide", None), P("wide")),
        check_vma=False,
    )
```

```python
import functools

import jax
import jax.numpy as jnp
from jax import lax
from jax.experimental import pallas as pl
from jax.experimental.pallas import tpu as pltpu
from jax.sharding import PartitionSpec as P

TILE = 128
STRATA = 2
BATCH = 4
GROUPS = 4
CHUNKS = 8
LAG_POS = 3
LAG_NEG = 4
ADD_FROM = (2, 3)
EARLY = 8
WINDOW = TILE + 16
MESH = pl.DeviceIdType.MESH
step_rate = 0.25
f32 = jnp.float32
bf16 = jnp.bfloat16
VMEM = pltpu.MemorySpace.VMEM
SMEM = pltpu.MemorySpace.SMEM


def dot(a, b, dims):
    return lax.dot_general(a, b, (dims, ((), ())), preferred_element_type=f32)


def pair(x):
    high = x.astype(bf16)
    low = (x - high.astype(f32)).astype(bf16)
    return jnp.concatenate([high, low], axis=0)


def tiles_kernel(
    stratum, ids, count, offsets, positives, users, state, block, negatives,
    new_users, new_state, pos_grad, neg_grad, split, square, padded, spread,
):
    cols = block.shape[0] // TILE
    rows = users.shape[0] // TILE
    side = TILE
    width = users.shape[1]
    new_users[...] = jnp.zeros(new_users.shape, f32)
    pos_grad[...] = jnp.zeros(pos_grad.shape, f32)
    spread[...] = jnp.zeros(spread.shape, f32)
    length = negatives.shape[0]
    padded[0:length, :] = negatives[...]
    padded[length:, :] = jnp.zeros((padded.shape[0] - length, width), f32)
    for col in range(cols):
        split[col] = pair(block[col * side : (col + 1) * side, :])
    live_count = count[0, stratum]
    item = lax.broadcasted_iota(jnp.int32, (side, side), 0)
    place = lax.broadcasted_iota(jnp.int32, (side, WINDOW), 1)

    def batch(step, carry):
        work = []
        for lane in range(BATCH):
            slot = step * BATCH + lane
            tile = ids[stratum, slot]
            within = lax.rem(offsets[stratum, slot], 8)
            window = pl.ds(pl.multiple_of(offsets[stratum, slot] - within, 8), WINDOW)
            row = pl.multiple_of(lax.div(tile, cols) * side, side)
            col = lax.rem(tile, cols)
            live = jnp.where(slot < live_count, 1.0 / side, 0.0).astype(f32)
            factors = users[pl.ds(row, side), :]
            factors_low = factors.astype(bf16)
            neg_rows = padded[window, :].astype(bf16)
            hot = jnp.where(item == positives[stratum, pl.ds(slot, 1), :], 1.0, 0.0).astype(f32)
            hot_t = hot.T.astype(bf16)
            hot = hot.astype(bf16)
            pos_rows = dot(jnp.concatenate([hot_t, hot_t], axis=1), split[col], ((1,), (0,)))
            neg_score = dot(factors_low, neg_rows, ((1,), (1,)))
            pos_score = jnp.sum(factors * pos_rows, axis=-1, keepdims=True)
            chosen = jnp.logical_and(place >= within, place < within + side)
            coeffs = jnp.where(chosen, live, 0.0) / (1.0 + jnp.exp(pos_score - neg_score))
            totals = jnp.sum(coeffs, axis=-1, keepdims=True)
            coeffs_low = coeffs.astype(bf16)
            factor_grad = dot(coeffs_low, neg_rows, ((1,), (0,))) - totals * pos_rows
            positive = dot(
                jnp.concatenate([hot, hot], axis=1), pair(totals * factors), ((1,), (0,))
            )
            coeffs_t = coeffs.T.astype(bf16)
            negative = dot(
                jnp.concatenate([coeffs_t, coeffs_t], axis=1), pair(factors), ((1,), (0,))
            )
            work.append((row, col, window, factor_grad, positive, negative))
        for row, col, window, factor_grad, positive, negative in work:
            new_users[pl.ds(row, side), :] += factor_grad
            at = pl.ds(pl.multiple_of(col * side, side), side)
            pos_grad[at, :] -= positive
            spread[window, :] += negative
        return carry

    lax.fori_loop(0, lax.div(live_count + (BATCH - 1), BATCH), batch, 0)
    neg_grad[...] = spread[0:length, :]
    square[...] = jnp.zeros(square.shape, f32)
    square[0:rows, :] = state[...]
    sums = square[...].T
    for row in range(rows):
        at = slice(row * side, (row + 1) * side)
        grad = new_users[at, :]
        fresh = sums[:, row : row + 1] + jnp.sum(grad * grad, axis=-1, keepdims=True) * (1.0 / width)
        new_users[at, :] = users[at, :] - (step_rate / jnp.sqrt(fresh)) * grad
        square[:, row : row + 1] = fresh
    new_state[...] = square[...].T[0:rows, :]


def run_tiles(stratum, ids, count, offsets, positives, users, state, block, negatives):
    width = users.shape[1]
    cols = block.shape[0] // TILE
    return pl.pallas_call(
        functools.partial(tiles_kernel, stratum),
        out_shape=(
            jax.ShapeDtypeStruct(users.shape, f32),
            jax.ShapeDtypeStruct(state.shape, f32),
            jax.ShapeDtypeStruct(block.shape, f32),
            jax.ShapeDtypeStruct(block.shape, f32),
        ),
        in_specs=[pl.BlockSpec(memory_space=SMEM)] * 3 + [pl.BlockSpec(memory_space=VMEM)] * 5,
        out_specs=(pl.BlockSpec(memory_space=VMEM),) * 4,
        scratch_shapes=[
            pltpu.VMEM((cols, 2 * TILE, width), bf16),
            pltpu.VMEM((TILE, TILE), f32),
            pltpu.VMEM((block.shape[0] + 16, width), f32),
            pltpu.VMEM((block.shape[0] + 16, width), f32),
        ],
        compiler_params=pltpu.CompilerParams(vmem_limit_bytes=24 * 1024 * 1024),
        name="tiles",
    )(ids, count, offsets, positives, users, state, block, negatives)


def greet(devices):
    barrier = pltpu.get_barrier_semaphore()
    for device in devices:
        pl.semaphore_signal(barrier, inc=1, device_id=device, device_id_type=MESH)
    pl.semaphore_wait(barrier, len(devices))


def start_remote(src, dst, sems, kind, chunk, device):
    copy = pltpu.make_async_remote_copy(
        src_ref=src,
        dst_ref=dst,
        send_sem=sems.at[0, kind, chunk],
        recv_sem=sems.at[1, kind, chunk],
        device_id=device,
        device_id_type=MESH,
    )
    copy.start()
    return copy


def whole_kernel(
    wide, users_hbm, user_state_hbm, items_hbm, item_state_hbm, ids_hbm, positives_hbm, count_hbm,
    offsets_hbm,
    new_users, new_user_state, new_items, new_item_state,
    users, high, low, user_state, block, block_next, item_state, positives, split, negs, negs_low,
    coeffs, pos_rows, neg_grad, beside_neg, summed, far, pos_grad, beside_pos, pos_sum, home_pos,
    fresh, factor_grad, pos_part, hot_t, square, columns, user_sums, item_sums, scores, totals, partial,
    ids, count, offsets, slot_of, sems, local_sems,
):
    w, r = lax.axis_index("wide"), lax.axis_index("narrow")
    slots = ids.shape[1]
    rows, side, width = users.shape
    cols = block.shape[0] // side
    half = block.shape[0] // 2
    size = half // CHUNKS
    per = CHUNKS // GROUPS
    quarter = half // GROUPS

    def at(shift):
        return (lax.rem(w + shift + wide, wide), r)

    across, ahead, behind = at(wide // 2), at(1), at(-1)
    far_ahead, far_behind = at(wide // 2 + 1), at(wide // 2 - 1)
    beside = (w, 1 - r)
    greet([beside, across, ahead, behind, far_ahead, far_behind])

    def span(which, chunk):
        return pl.ds(pl.multiple_of(which * half + chunk * size, size), size)

    def inner(which, chunk):
        return pl.ds(pl.multiple_of(which * quarter + (chunk % per) * size, size), size)

    def local(chunk):
        return slice(chunk * size, (chunk + 1) * size)

    started = []

    def send(src, dst, kind, chunk, device):
        copy = start_remote(src, dst, sems, kind, chunk, device)
        started.append(copy)
        return copy

    def neg_at(stratum, which, chunk):
        return negs.at[stratum, chunk // per, inner(which, chunk), :]

    arriving = [
        send(items_hbm.at[span(r, c), :], neg_at(0, r, c), 0, c, across) for c in range(CHUNKS)
    ]
    loads = []
    for k, (src, dst) in enumerate(
        [
            (ids_hbm, ids), (count_hbm, count), (offsets_hbm, offsets), (positives_hbm, positives),
            (items_hbm, block), (users_hbm, users), (user_state_hbm, user_state),
            (item_state_hbm, item_state),
        ]
    ):
        loads.append(pltpu.make_async_copy(src, dst, local_sems.at[k]))
        loads[-1].start()
    factor_grad[slots] = jnp.zeros((side, width), f32)
    pos_part[slots] = jnp.zeros((side, width), f32)
    columns[...] = jnp.zeros(columns.shape, f32)
    square[...] = jnp.zeros(square.shape, f32)
    for load in loads:
        load.wait()

    item = lax.broadcasted_iota(jnp.int32, (side, side), 0)

    def find(tile, carry):
        for stratum in range(STRATA):
            found = jnp.int32(slots)
            for slot in range(slots):
                found = jnp.where(ids[stratum, slot] == tile, jnp.int32(slot), found)
            slot_of[stratum, tile] = found
        return carry

    def hots(stratum):
        for slot in range(slots):
            hot = jnp.where(item == positives[stratum, slot : slot + 1, :], 1.0, 0.0).astype(f32)
            hot_t[stratum, slot] = hot.T.astype(bf16)

    def split_users(source):
        def step(row, carry):
            value = source[row]
            top = value.astype(bf16)
            high[row] = top
            low[row] = (value - top.astype(f32)).astype(bf16)
            return carry

        lax.fori_loop(0, rows, step, 0)

    def row_at(stratum, slot):
        return lax.div(ids[stratum, slot], cols)

    def prepare(stratum, source, own):
        for col in range(cols):
            split[col] = pair(own[col * side : (col + 1) * side, :])

        for slot in range(slots):
            hot = hot_t[stratum, slot]
            picked = dot(
                jnp.concatenate([hot, hot], axis=1),
                split[lax.rem(ids[stratum, slot], cols)],
                ((1,), (0,)),
            )
            pos_rows[slot] = picked
            columns[:, slot : slot + 1] = jnp.sum(
                source[row_at(stratum, slot)] * picked, axis=-1, keepdims=True
            )
        scores[...] = columns[...].T
        partial[...] = jnp.zeros(partial.shape, f32)

    def group(stratum, g):
        near = negs[stratum, g].astype(bf16)
        here = slice(g * side, (g + 1) * side)
        negs_low[here, :] = near
        index = item + jnp.where(item >= quarter, half - quarter, 0) + g * quarter

        weights, tops, lows = [], [], []
        for slot in range(slots):
            top = high[row_at(stratum, slot)]
            scale = jnp.where(slot < count[0, stratum], 0.5 / side, 0.0).astype(f32)
            score = dot(near, top, ((1,), (1,)))
            place = index - offsets[stratum, slot]
            chosen = jnp.logical_and(place >= 0, place < side)
            part = jnp.where(chosen, scale, 0.0)
            part += part * jnp.tanh(0.5 * (score - scores[slot : slot + 1, :]))
            partial[slot] += jnp.sum(part.reshape(side // 8, 8, side), axis=0)
            part = part.astype(bf16)
            coeffs[slot, here, :] = part
            weights.append(part)
            tops.append(top)
            lows.append(low[row_at(stratum, slot)])
        left = jnp.concatenate(weights, axis=1)
        neg_grad[stratum, g] = dot(left, jnp.concatenate(tops, axis=0), ((1,), (0,))) + dot(
            left, jnp.concatenate(lows, axis=0), ((1,), (0,))
        )

    def add_totals():
        square[0:slots, :] = jnp.sum(partial[...], axis=1)
        totals[...] = square[...].T

    def positive_part(stratum, slot):
        chosen = item == positives[stratum, slot : slot + 1, :]
        hot = jnp.where(chosen, square[slot : slot + 1, :], 0.0)
        top = hot.astype(bf16)
        rest = (hot - top.astype(f32)).astype(bf16)
        upper, lower = high[row_at(stratum, slot)], low[row_at(stratum, slot)]
        pos_part[slot] = dot(
            jnp.concatenate([top, rest], axis=1),
            jnp.concatenate([upper, upper], axis=0),
            ((1,), (0,)),
        ) + dot(top, lower, ((1,), (0,)))

    def positive(stratum, which):
        for k in range(cols // 2):
            col = which * (cols // 2) + k
            total = pos_part[slot_of[stratum, col]]
            for row in range(1, rows):
                total += pos_part[slot_of[stratum, row * cols + col]]
            pos_grad[stratum, pl.ds(pl.multiple_of(col * side, side), side), :] = -total

    def factor_part(slot):
        factor_grad[slot] = (
            dot(coeffs[slot], negs_low[...], ((0,), (0,)))
            - totals[:, slot : slot + 1] * pos_rows[slot]
        )

    def update_part(stratum, row, source, last):
        grad = factor_grad[slot_of[stratum, row * cols]]
        for col in range(1, cols):
            grad += factor_grad[slot_of[stratum, row * cols + col]]
        sums = user_sums[:, row : row + 1] + jnp.sum(grad * grad, axis=-1, keepdims=True) * (
            1.0 / width
        )
        value = source[row] - (step_rate / jnp.sqrt(sums)) * grad
        user_sums[:, row : row + 1] = sums
        new_users[row] = value
        if not last:
            top = value.astype(bf16)
            high[row] = top
            low[row] = (value - top.astype(f32)).astype(bf16)

    def user_work(stratum, source, last):
        for slot in range(slots):
            yield functools.partial(factor_part, slot)
        for row in range(rows):
            yield functools.partial(update_part, stratum, row, source, last)

    def adagrad(stratum, c, grad, value):
        col, begin = c * size // side, c * size % side
        sums = item_sums[begin : begin + size, col : col + 1] + jnp.sum(
            grad * grad, axis=-1, keepdims=True
        ) * (1.0 / width)
        item_sums[begin : begin + size, col : col + 1] = sums
        return value - (step_rate / jnp.sqrt(sums)) * grad

    square[0:rows, :] = user_state[...]
    user_sums[...] = square[...].T
    square[0 : half // side, :] = item_state[r]
    item_sums[...] = square[...].T
    hots(0)
    split_users(users)
    prepare(0, users, block)

    def chunks_of(g):
        return range(g * per, (g + 1) * per)

    def work_through(stratum, arriving, relayed, kind, target):
        side_neg, out = [], []

        def relay(c):
            arriving[c].wait_recv()
            relayed.append(send(neg_at(stratum, r, c), neg_at(stratum, r, c), kind, c, beside))

        def add(g):
            for c in chunks_of(g):
                side_neg[c].wait_recv()
                summed[stratum, local(c), :] = (
                    neg_grad[stratum, g, inner(r, c), :] + beside_neg[stratum, local(c), :]
                )
                out.append(
                    send(
                        summed.at[stratum, local(c), :], far.at[stratum, local(c), :],
                        kind + 2, c, target,
                    )
                )

        for g in range(GROUPS):
            for c in range(len(relayed), (g + 1) * per):
                relay(c)
            for c in chunks_of(g):
                relayed[c].wait_recv()
            if g + 1 < GROUPS:
                for c in range(len(relayed), (g + 2) * per):
                    relay(c)
            group(stratum, g)
            for c in chunks_of(g):
                side_neg.append(
                    send(
                        neg_grad.at[stratum, g, inner(1 - r, c), :],
                        beside_neg.at[stratum, local(c), :],
                        kind + 1, c, beside,
                    )
                )
            if g >= ADD_FROM[stratum]:
                add(g - ADD_FROM[stratum])
        add_totals()
        for slot in range(slots):
            positive_part(stratum, slot)
        positive(stratum, 1 - r)
        side_pos = [
            send(
                pos_grad.at[stratum, span(1 - r, c), :], beside_pos.at[stratum, local(c), :],
                kind + 3, c, beside,
            )
            for c in range(CHUNKS)
        ]
        for g in range(GROUPS - ADD_FROM[stratum], GROUPS):
            add(g)
        positive(stratum, r)
        return out, side_pos

    lax.fori_loop(0, rows * cols, find, 0)
    hots(1)
    out, side_pos = work_through(0, arriving, [], 1, across)
    work = list(user_work(0, users, False))
    pieces = CHUNKS + LAG_POS
    arriving, passed, relayed, shared = [], [], [], []
    for step in range(EARLY + LAG_NEG):
        for piece in work[len(work) * step // pieces : len(work) * (step + 1) // pieces]:
            piece()
        if step < CHUNKS:
            c = step
            side_pos[c].wait_recv()
            out[c].wait_recv()
            grad = pos_grad[0, span(r, c), :] + beside_pos[0, local(c), :] + far[0, local(c), :]
            fresh[local(c), :] = adagrad(0, c, grad, block[span(r, c), :])
            arriving.append(send(fresh.at[local(c), :], neg_at(1, r, c), 5, c, far_ahead))
            passed.append(send(fresh.at[local(c), :], block_next.at[span(r, c), :], 6, c, ahead))
        if 0 <= step - LAG_POS < CHUNKS:
            c = step - LAG_POS
            passed[c].wait_recv()
            shared.append(
                send(block_next.at[span(r, c), :], block_next.at[span(r, c), :], 7, c, beside)
            )
        if 0 <= step - LAG_NEG < EARLY:
            c = step - LAG_NEG
            arriving[c].wait_recv()
            relayed.append(send(neg_at(1, r, c), neg_at(1, r, c), 8, c, beside))
    for c in range(CHUNKS):
        shared[c].wait_recv()
    prepare(1, new_users, block_next)
    out, side_pos = work_through(1, arriving, relayed, 8, far_behind)
    homeward, last = [], []
    work = list(user_work(1, new_users, True))
    steps = 2 * CHUNKS
    for step in range(steps):
        for piece in work[len(work) * step // steps : len(work) * (step + 1) // steps]:
            piece()
        c = step % CHUNKS
        if step < CHUNKS:
            side_pos[c].wait_recv()
            pos_sum[local(c), :] = pos_grad[1, span(r, c), :] + beside_pos[1, local(c), :]
            homeward.append(send(pos_sum.at[local(c), :], home_pos.at[local(c), :], 12, c, behind))
        else:
            homeward[c].wait_recv()
            out[c].wait_recv()
            grad = home_pos[local(c), :] + far[1, local(c), :]
            new_items[span(r, c), :] = adagrad(1, c, grad, fresh[local(c), :])
            here = new_items.at[span(r, c), :]
            last.append(send(here, here, 13, c, beside))
    new_user_state[...] = user_sums[...].T[0:rows, :]
    new_item_state[r] = item_sums[...].T[0 : half // side, :]
    last.append(send(new_item_state.at[r], new_item_state.at[r], 14, 0, beside))
    for copy in last:
        copy.wait_recv()
    for copy in started:
        copy.wait_send()


def run_whole(users, user_state, items, item_state, ids, positives, count, offsets):
    block, width = items.shape
    half = block // 2
    slots = ids.shape[1]
    cols = block // TILE
    tiles = users.shape[0] * cols
    arrays = (users, user_state, items, item_state, ids, positives, count, offsets)
    hbm = pltpu.MemorySpace.HBM
    square = pltpu.VMEM((TILE, TILE), f32)
    results = pl.pallas_call(
        functools.partial(whole_kernel, lax.axis_size("wide")),
        out_shape=[jax.ShapeDtypeStruct(a.shape, f32) for a in arrays[:4]],
        in_specs=[pl.BlockSpec(memory_space=hbm)] * len(arrays),
        out_specs=[pl.BlockSpec(memory_space=VMEM)] * 4,
        scratch_shapes=[
            pltpu.VMEM(users.shape, f32),
            pltpu.VMEM(users.shape, bf16),
            pltpu.VMEM(users.shape, bf16),
            pltpu.VMEM(user_state.shape, f32),
            pltpu.VMEM(items.shape, f32),
            pltpu.VMEM(items.shape, f32),
            pltpu.VMEM(item_state.shape, f32),
            pltpu.VMEM(positives.shape, jnp.int32),
            pltpu.VMEM((cols, 2 * TILE, width), bf16),
            pltpu.VMEM((STRATA, GROUPS, TILE, width), f32),
            pltpu.VMEM(items.shape, bf16),
            pltpu.VMEM((slots, block, TILE), bf16),
            pltpu.VMEM((slots, TILE, width), f32),
            pltpu.VMEM((STRATA, GROUPS, TILE, width), f32),
            pltpu.VMEM((STRATA, half, width), f32),
            pltpu.VMEM((STRATA, half, width), f32),
            pltpu.VMEM((STRATA, half, width), f32),
            pltpu.VMEM((STRATA, block, width), f32),
            pltpu.VMEM((STRATA, half, width), f32),
            pltpu.VMEM((half, width), f32),
            pltpu.VMEM((half, width), f32),
            pltpu.VMEM((half, width), f32),
            pltpu.VMEM((slots + 1, TILE, width), f32),
            pltpu.VMEM((slots + 1, TILE, width), f32),
            pltpu.VMEM((STRATA, slots, TILE, TILE), bf16),
            square, square, square, square, square, square,
            pltpu.VMEM((slots, 8, TILE), f32),
            pltpu.SMEM(ids.shape, jnp.int32),
            pltpu.SMEM(count.shape, jnp.int32),
            pltpu.SMEM(offsets.shape, jnp.int32),
            pltpu.SMEM((STRATA, tiles), jnp.int32),
            pltpu.SemaphoreType.DMA((2, 15, CHUNKS)),
            pltpu.SemaphoreType.DMA((len(arrays),)),
        ],
        compiler_params=pltpu.CompilerParams(
            collective_id=0, has_side_effects=True, vmem_limit_bytes=40 * 1024 * 1024
        ),
        name="whole",
    )(*[pltpu.with_memory_space_constraint(a, hbm) for a in arrays])
    return write_results(results)


def results_kernel(count, *refs):
    sems = refs[-1]
    copies = [
        pltpu.make_async_copy(refs[k], refs[count + k], sems.at[k]) for k in range(count)
    ]
    for copy in copies:
        copy.start()
    for copy in copies:
        copy.wait()


def write_results(arrays):
    count = len(arrays)
    return pl.pallas_call(
        functools.partial(results_kernel, count),
        out_shape=[jax.ShapeDtypeStruct(a.shape, a.dtype) for a in arrays],
        in_specs=[pl.BlockSpec(memory_space=VMEM)] * count,
        out_specs=[pl.BlockSpec(memory_space=pltpu.MemorySpace.HBM)] * count,
        scratch_shapes=[pltpu.SemaphoreType.DMA((count,))],
        compiler_params=pltpu.CompilerParams(vmem_limit_bytes=1024 * 1024),
        name="results",
    )(*arrays)


def passed_along(block, distance):
    size = lax.axis_size("wide")
    return lax.ppermute(block, "wide", [((i - distance) % size, i) for i in range(size)])


def general_exchange(shift, pos_grad, neg_grad, block, state):
    half = lax.axis_size("wide") // 2
    total = lax.psum(pos_grad + passed_along(neg_grad, half), "narrow")
    new_state = state + jnp.mean(total * total, axis=-1)
    block = block - step_rate * total / jnp.sqrt(new_state)[:, None]
    return passed_along((block, new_state), shift)


def per_device(users, user_state, items, item_state, tile_ids, tile_count, pos_items, neg_offsets):
    wide, narrow = lax.axis_size("wide"), lax.axis_size("narrow")
    ids, count = tile_ids[0, 0], tile_count[0]
    positives, offsets = pos_items[0, 0], neg_offsets[0, 0]
    own_state = user_state.reshape(-1, TILE)
    if narrow == 2:
        users, own_state, block, block_state = run_whole(
            users.reshape(-1, TILE, users.shape[1]), own_state, items, item_state.reshape(2, -1, TILE), ids, positives, count, offsets
        )
    else:
        block, block_state = items, item_state
        for stratum in range(STRATA):
            negatives = passed_along(block, wide // 2)
            users, own_state, pos_grad, neg_grad = run_tiles(
                stratum, ids, count, offsets, positives, users, own_state, block, negatives
            )
            shift = 1 - STRATA if stratum + 1 == STRATA else 1
            block, block_state = general_exchange(shift, pos_grad, neg_grad, block, block_state)
    return (users.reshape(-1, users.shape[-1]), own_state.reshape(user_state.shape), block, block_state.reshape(item_state.shape))


def solution(mesh):
    return jax.shard_map(
        per_device,
        mesh=mesh,
        in_specs=(
            P(("wide", "narrow"), None),
            P(("wide", "narrow")),
            P("wide", None),
            P("wide"),
            P("wide", "narrow", None, None),
            P("wide", "narrow", None),
            P("wide", "narrow", None, None, None),
            P("wide", "narrow", None, None),
        ),
        out_specs=(P(("wide", "narrow"), None), P(("wide", "narrow")), P("wide", None), P("wide")),
        check_vma=False,
    )
```

```python
import functools

import jax
import jax.numpy as jnp
from jax import lax
from jax.experimental import pallas as pl
from jax.experimental.pallas import tpu as pltpu
from jax.sharding import PartitionSpec as P

TILE = 128
STRATA = 2
BATCH = 4
GROUPS = 4
CHUNKS = 8
LAG_POS = 3
LAG_NEG = 4
ADD_FROM = (2, 3)
EARLY = 8
WINDOW = TILE + 16
MESH = pl.DeviceIdType.MESH
step_rate = 0.25
f32 = jnp.float32
bf16 = jnp.bfloat16
VMEM = pltpu.MemorySpace.VMEM
SMEM = pltpu.MemorySpace.SMEM


def dot(a, b, dims):
    return lax.dot_general(a, b, (dims, ((), ())), preferred_element_type=f32)


def pair(x):
    high = x.astype(bf16)
    low = (x - high.astype(f32)).astype(bf16)
    return jnp.concatenate([high, low], axis=0)


def tiles_kernel(
    stratum, ids, count, offsets, positives, users, state, block, negatives,
    new_users, new_state, pos_grad, neg_grad, split, square, padded, spread,
):
    cols = block.shape[0] // TILE
    rows = users.shape[0] // TILE
    side = TILE
    width = users.shape[1]
    new_users[...] = jnp.zeros(new_users.shape, f32)
    pos_grad[...] = jnp.zeros(pos_grad.shape, f32)
    spread[...] = jnp.zeros(spread.shape, f32)
    length = negatives.shape[0]
    padded[0:length, :] = negatives[...]
    padded[length:, :] = jnp.zeros((padded.shape[0] - length, width), f32)
    for col in range(cols):
        split[col] = pair(block[col * side : (col + 1) * side, :])
    live_count = count[0, stratum]
    item = lax.broadcasted_iota(jnp.int32, (side, side), 0)
    place = lax.broadcasted_iota(jnp.int32, (side, WINDOW), 1)

    def batch(step, carry):
        work = []
        for lane in range(BATCH):
            slot = step * BATCH + lane
            tile = ids[stratum, slot]
            within = lax.rem(offsets[stratum, slot], 8)
            window = pl.ds(pl.multiple_of(offsets[stratum, slot] - within, 8), WINDOW)
            row = pl.multiple_of(lax.div(tile, cols) * side, side)
            col = lax.rem(tile, cols)
            live = jnp.where(slot < live_count, 1.0 / side, 0.0).astype(f32)
            factors = users[pl.ds(row, side), :]
            factors_low = factors.astype(bf16)
            neg_rows = padded[window, :].astype(bf16)
            hot = jnp.where(item == positives[stratum, pl.ds(slot, 1), :], 1.0, 0.0).astype(f32)
            hot_t = hot.T.astype(bf16)
            hot = hot.astype(bf16)
            pos_rows = dot(jnp.concatenate([hot_t, hot_t], axis=1), split[col], ((1,), (0,)))
            neg_score = dot(factors_low, neg_rows, ((1,), (1,)))
            pos_score = jnp.sum(factors * pos_rows, axis=-1, keepdims=True)
            chosen = jnp.logical_and(place >= within, place < within + side)
            coeffs = jnp.where(chosen, live, 0.0) / (1.0 + jnp.exp(pos_score - neg_score))
            totals = jnp.sum(coeffs, axis=-1, keepdims=True)
            coeffs_low = coeffs.astype(bf16)
            factor_grad = dot(coeffs_low, neg_rows, ((1,), (0,))) - totals * pos_rows
            positive = dot(
                jnp.concatenate([hot, hot], axis=1), pair(totals * factors), ((1,), (0,))
            )
            coeffs_t = coeffs.T.astype(bf16)
            negative = dot(
                jnp.concatenate([coeffs_t, coeffs_t], axis=1), pair(factors), ((1,), (0,))
            )
            work.append((row, col, window, factor_grad, positive, negative))
        for row, col, window, factor_grad, positive, negative in work:
            new_users[pl.ds(row, side), :] += factor_grad
            at = pl.ds(pl.multiple_of(col * side, side), side)
            pos_grad[at, :] -= positive
            spread[window, :] += negative
        return carry

    lax.fori_loop(0, lax.div(live_count + (BATCH - 1), BATCH), batch, 0)
    neg_grad[...] = spread[0:length, :]
    square[...] = jnp.zeros(square.shape, f32)
    square[0:rows, :] = state[...]
    sums = square[...].T
    for row in range(rows):
        at = slice(row * side, (row + 1) * side)
        grad = new_users[at, :]
        fresh = sums[:, row : row + 1] + jnp.sum(grad * grad, axis=-1, keepdims=True) * (1.0 / width)
        new_users[at, :] = users[at, :] - (step_rate / jnp.sqrt(fresh)) * grad
        square[:, row : row + 1] = fresh
    new_state[...] = square[...].T[0:rows, :]


def run_tiles(stratum, ids, count, offsets, positives, users, state, block, negatives):
    width = users.shape[1]
    cols = block.shape[0] // TILE
    return pl.pallas_call(
        functools.partial(tiles_kernel, stratum),
        out_shape=(
            jax.ShapeDtypeStruct(users.shape, f32),
            jax.ShapeDtypeStruct(state.shape, f32),
            jax.ShapeDtypeStruct(block.shape, f32),
            jax.ShapeDtypeStruct(block.shape, f32),
        ),
        in_specs=[pl.BlockSpec(memory_space=SMEM)] * 3 + [pl.BlockSpec(memory_space=VMEM)] * 5,
        out_specs=(pl.BlockSpec(memory_space=VMEM),) * 4,
        scratch_shapes=[
            pltpu.VMEM((cols, 2 * TILE, width), bf16),
            pltpu.VMEM((TILE, TILE), f32),
            pltpu.VMEM((block.shape[0] + 16, width), f32),
            pltpu.VMEM((block.shape[0] + 16, width), f32),
        ],
        compiler_params=pltpu.CompilerParams(vmem_limit_bytes=24 * 1024 * 1024),
        name="tiles",
    )(ids, count, offsets, positives, users, state, block, negatives)


def greet(devices):
    barrier = pltpu.get_barrier_semaphore()
    for device in devices:
        pl.semaphore_signal(barrier, inc=1, device_id=device, device_id_type=MESH)
    pl.semaphore_wait(barrier, len(devices))


def start_remote(src, dst, sems, kind, chunk, device):
    copy = pltpu.make_async_remote_copy(
        src_ref=src,
        dst_ref=dst,
        send_sem=sems.at[0, kind, chunk],
        recv_sem=sems.at[1, kind, chunk],
        device_id=device,
        device_id_type=MESH,
    )
    copy.start()
    return copy


def whole_kernel(
    wide, users_hbm, user_state_hbm, items_hbm, item_state_hbm, ids_hbm, positives_hbm, count_hbm,
    offsets_hbm,
    new_users, new_user_state, new_items, new_item_state,
    users, high, low, user_state, block, block_next, item_state, positives, split, negs, negs_low,
    coeffs, pos_rows, neg_grad, beside_neg, summed, far, pos_grad, beside_pos, pos_sum, home_pos,
    fresh, factor_grad, pos_part, hot_t, square, columns, user_sums, item_sums, scores, totals, partial,
    ids, count, offsets, slot_of, sems, local_sems,
):
    w, r = lax.axis_index("wide"), lax.axis_index("narrow")
    slots = ids.shape[1]
    rows, side, width = users.shape
    cols = block.shape[0] // side
    half = block.shape[0] // 2
    size = half // CHUNKS
    per = CHUNKS // GROUPS
    quarter = half // GROUPS

    def at(shift):
        return (lax.rem(w + shift + wide, wide), r)

    across, ahead, behind = at(wide // 2), at(1), at(-1)
    far_ahead, far_behind = at(wide // 2 + 1), at(wide // 2 - 1)
    beside = (w, 1 - r)
    greet([beside, across, ahead, behind, far_ahead, far_behind])

    def span(which, chunk):
        return pl.ds(pl.multiple_of(which * half + chunk * size, size), size)

    def inner(which, chunk):
        return pl.ds(pl.multiple_of(which * quarter + (chunk % per) * size, size), size)

    def local(chunk):
        return slice(chunk * size, (chunk + 1) * size)

    started = []

    def send(src, dst, kind, chunk, device):
        copy = start_remote(src, dst, sems, kind, chunk, device)
        started.append(copy)
        return copy

    def neg_at(stratum, which, chunk):
        return negs.at[stratum, chunk // per, inner(which, chunk), :]

    arriving = [
        send(items_hbm.at[span(r, c), :], neg_at(0, r, c), 0, c, across) for c in range(CHUNKS)
    ]
    loads = []
    for k, (src, dst) in enumerate(
        [
            (ids_hbm, ids), (count_hbm, count), (offsets_hbm, offsets), (positives_hbm, positives),
            (items_hbm, block), (users_hbm, users), (user_state_hbm, user_state),
            (item_state_hbm, item_state),
        ]
    ):
        loads.append(pltpu.make_async_copy(src, dst, local_sems.at[k]))
        loads[-1].start()
    factor_grad[slots] = jnp.zeros((side, width), f32)
    pos_part[slots] = jnp.zeros((side, width), f32)
    columns[...] = jnp.zeros(columns.shape, f32)
    square[...] = jnp.zeros(square.shape, f32)
    for load in loads:
        load.wait()

    item = lax.broadcasted_iota(jnp.int32, (side, side), 0)

    def find(tile, carry):
        for stratum in range(STRATA):
            found = jnp.int32(slots)
            for slot in range(slots):
                found = jnp.where(ids[stratum, slot] == tile, jnp.int32(slot), found)
            slot_of[stratum, tile] = found
        return carry

    def hots(stratum):
        for slot in range(slots):
            hot = jnp.where(item == positives[stratum, slot : slot + 1, :], 1.0, 0.0).astype(f32)
            hot_t[stratum, slot] = hot.T.astype(bf16)

    def split_users(source):
        def step(row, carry):
            value = source[row]
            top = value.astype(bf16)
            high[row] = top
            low[row] = (value - top.astype(f32)).astype(bf16)
            return carry

        lax.fori_loop(0, rows, step, 0)

    def row_at(stratum, slot):
        return lax.div(ids[stratum, slot], cols)

    def prepare(stratum, source, own):
        for col in range(cols):
            split[col] = pair(own[col * side : (col + 1) * side, :])

        for slot in range(slots):
            hot = hot_t[stratum, slot]
            picked = dot(
                jnp.concatenate([hot, hot], axis=1),
                split[lax.rem(ids[stratum, slot], cols)],
                ((1,), (0,)),
            )
            pos_rows[slot] = picked
            columns[:, slot : slot + 1] = jnp.sum(
                source[row_at(stratum, slot)] * picked, axis=-1, keepdims=True
            )
        scores[...] = columns[...].T
        partial[...] = jnp.zeros(partial.shape, f32)

    def group(stratum, g):
        near = negs[stratum, g].astype(bf16)
        here = slice(g * side, (g + 1) * side)
        negs_low[here, :] = near
        index = item + jnp.where(item >= quarter, half - quarter, 0) + g * quarter

        weights, tops, lows = [], [], []
        for slot in range(slots):
            top = high[row_at(stratum, slot)]
            scale = jnp.where(slot < count[0, stratum], 0.5 / side, 0.0).astype(f32)
            score = dot(near, top, ((1,), (1,)))
            place = index - offsets[stratum, slot]
            chosen = jnp.logical_and(place >= 0, place < side)
            part = jnp.where(chosen, scale, 0.0)
            part += part * jnp.tanh(0.5 * (score - scores[slot : slot + 1, :]))
            partial[slot] += jnp.sum(part.reshape(side // 8, 8, side), axis=0)
            part = part.astype(bf16)
            coeffs[slot, here, :] = part
            weights.append(part)
            tops.append(top)
            lows.append(low[row_at(stratum, slot)])
        left = jnp.concatenate(weights, axis=1)
        neg_grad[stratum, g] = dot(left, jnp.concatenate(tops, axis=0), ((1,), (0,))) + dot(
            left, jnp.concatenate(lows, axis=0), ((1,), (0,))
        )

    def add_totals():
        square[0:slots, :] = jnp.sum(partial[...], axis=1)
        totals[...] = square[...].T

    def positive_part(stratum, slot):
        chosen = item == positives[stratum, slot : slot + 1, :]
        hot = jnp.where(chosen, square[slot : slot + 1, :], 0.0)
        top = hot.astype(bf16)
        rest = (hot - top.astype(f32)).astype(bf16)
        upper, lower = high[row_at(stratum, slot)], low[row_at(stratum, slot)]
        pos_part[slot] = dot(
            jnp.concatenate([top, rest], axis=1),
            jnp.concatenate([upper, upper], axis=0),
            ((1,), (0,)),
        ) + dot(top, lower, ((1,), (0,)))

    def positive(stratum, which):
        for k in range(cols // 2):
            col = which * (cols // 2) + k
            total = pos_part[slot_of[stratum, col]]
            for row in range(1, rows):
                total += pos_part[slot_of[stratum, row * cols + col]]
            pos_grad[stratum, pl.ds(pl.multiple_of(col * side, side), side), :] = -total

    def factor_part(slot):
        factor_grad[slot] = (
            dot(coeffs[slot], negs_low[...], ((0,), (0,)))
            - totals[:, slot : slot + 1] * pos_rows[slot]
        )

    def update_part(stratum, row, source, last):
        grad = factor_grad[slot_of[stratum, row * cols]]
        for col in range(1, cols):
            grad += factor_grad[slot_of[stratum, row * cols + col]]
        sums = user_sums[:, row : row + 1] + jnp.sum(grad * grad, axis=-1, keepdims=True) * (
            1.0 / width
        )
        value = source[row] - (step_rate / jnp.sqrt(sums)) * grad
        user_sums[:, row : row + 1] = sums
        new_users[row] = value
        if not last:
            top = value.astype(bf16)
            high[row] = top
            low[row] = (value - top.astype(f32)).astype(bf16)

    def user_work(stratum, source, last):
        for slot in range(slots):
            yield functools.partial(factor_part, slot)
        for row in range(rows):
            yield functools.partial(update_part, stratum, row, source, last)

    def adagrad(stratum, c, grad, value):
        col, begin = c * size // side, c * size % side
        sums = item_sums[begin : begin + size, col : col + 1] + jnp.sum(
            grad * grad, axis=-1, keepdims=True
        ) * (1.0 / width)
        item_sums[begin : begin + size, col : col + 1] = sums
        return value - (step_rate / jnp.sqrt(sums)) * grad

    square[0:rows, :] = user_state[...]
    user_sums[...] = square[...].T
    square[0 : half // side, :] = item_state[r]
    item_sums[...] = square[...].T
    hots(0)
    split_users(users)
    prepare(0, users, block)

    def chunks_of(g):
        return range(g * per, (g + 1) * per)

    def work_through(stratum, arriving, relayed, kind, target):
        side_neg, out = [], []

        def relay(c):
            arriving[c].wait_recv()
            relayed.append(send(neg_at(stratum, r, c), neg_at(stratum, r, c), kind, c, beside))

        def add(g):
            for c in chunks_of(g):
                side_neg[c].wait_recv()
                summed[stratum, local(c), :] = (
                    neg_grad[stratum, g, inner(r, c), :] + beside_neg[stratum, local(c), :]
                )
                out.append(
                    send(
                        summed.at[stratum, local(c), :], far.at[stratum, local(c), :],
                        kind + 2, c, target,
                    )
                )

        for g in range(GROUPS):
            for c in range(len(relayed), (g + 1) * per):
                relay(c)
            for c in chunks_of(g):
                relayed[c].wait_recv()
            if g + 1 < GROUPS:
                for c in range(len(relayed), (g + 2) * per):
                    relay(c)
            group(stratum, g)
            for c in chunks_of(g):
                side_neg.append(
                    send(
                        neg_grad.at[stratum, g, inner(1 - r, c), :],
                        beside_neg.at[stratum, local(c), :],
                        kind + 1, c, beside,
                    )
                )
            if g >= ADD_FROM[stratum]:
                add(g - ADD_FROM[stratum])
        add_totals()
        for slot in range(slots):
            positive_part(stratum, slot)
        positive(stratum, 1 - r)
        side_pos = [
            send(
                pos_grad.at[stratum, span(1 - r, c), :], beside_pos.at[stratum, local(c), :],
                kind + 3, c, beside,
            )
            for c in range(CHUNKS)
        ]
        for g in range(GROUPS - ADD_FROM[stratum], GROUPS):
            add(g)
        positive(stratum, r)
        return out, side_pos

    lax.fori_loop(0, rows * cols, find, 0)
    hots(1)
    out, side_pos = work_through(0, arriving, [], 1, across)
    work = list(user_work(0, users, False))
    pieces = CHUNKS + LAG_POS
    arriving, passed, relayed, shared = [], [], [], []
    for step in range(EARLY + LAG_NEG):
        for piece in work[len(work) * step // pieces : len(work) * (step + 1) // pieces]:
            piece()
        if step < CHUNKS:
            c = step
            side_pos[c].wait_recv()
            out[c].wait_recv()
            grad = pos_grad[0, span(r, c), :] + beside_pos[0, local(c), :] + far[0, local(c), :]
            fresh[local(c), :] = adagrad(0, c, grad, block[span(r, c), :])
            arriving.append(send(fresh.at[local(c), :], neg_at(1, r, c), 5, c, far_ahead))
            passed.append(send(fresh.at[local(c), :], block_next.at[span(r, c), :], 6, c, ahead))
        if 0 <= step - LAG_POS < CHUNKS:
            c = step - LAG_POS
            passed[c].wait_recv()
            shared.append(
                send(block_next.at[span(r, c), :], block_next.at[span(r, c), :], 7, c, beside)
            )
        if 0 <= step - LAG_NEG < EARLY:
            c = step - LAG_NEG
            arriving[c].wait_recv()
            relayed.append(send(neg_at(1, r, c), neg_at(1, r, c), 8, c, beside))
    for c in range(CHUNKS):
        shared[c].wait_recv()
    prepare(1, new_users, block_next)
    out, side_pos = work_through(1, arriving, relayed, 8, far_behind)
    homeward, last = [], []
    work = list(user_work(1, new_users, True))
    steps = 2 * CHUNKS
    for step in range(steps):
        for piece in work[len(work) * step // CHUNKS : len(work) * (step + 1) // CHUNKS]:
            piece()
        c = step % CHUNKS
        if step < CHUNKS:
            side_pos[c].wait_recv()
            pos_sum[local(c), :] = pos_grad[1, span(r, c), :] + beside_pos[1, local(c), :]
            homeward.append(send(pos_sum.at[local(c), :], home_pos.at[local(c), :], 12, c, behind))
            if c == CHUNKS - 1:
                new_user_state[...] = user_sums[...].T[0:rows, :]
        else:
            homeward[c].wait_recv()
            out[c].wait_recv()
            grad = home_pos[local(c), :] + far[1, local(c), :]
            new_items[span(r, c), :] = adagrad(1, c, grad, fresh[local(c), :])
            here = new_items.at[span(r, c), :]
            last.append(send(here, here, 13, c, beside))
    new_item_state[r] = item_sums[...].T[0 : half // side, :]
    last.append(send(new_item_state.at[r], new_item_state.at[r], 14, 0, beside))
    for copy in last:
        copy.wait_recv()
    for copy in started:
        copy.wait_send()


def run_whole(users, user_state, items, item_state, ids, positives, count, offsets):
    block, width = items.shape
    half = block // 2
    slots = ids.shape[1]
    cols = block // TILE
    tiles = users.shape[0] * cols
    arrays = (users, user_state, items, item_state, ids, positives, count, offsets)
    hbm = pltpu.MemorySpace.HBM
    square = pltpu.VMEM((TILE, TILE), f32)
    results = pl.pallas_call(
        functools.partial(whole_kernel, lax.axis_size("wide")),
        out_shape=[jax.ShapeDtypeStruct(a.shape, f32) for a in arrays[:4]],
        in_specs=[pl.BlockSpec(memory_space=hbm)] * len(arrays),
        out_specs=[pl.BlockSpec(memory_space=VMEM)] * 4,
        scratch_shapes=[
            pltpu.VMEM(users.shape, f32),
            pltpu.VMEM(users.shape, bf16),
            pltpu.VMEM(users.shape, bf16),
            pltpu.VMEM(user_state.shape, f32),
            pltpu.VMEM(items.shape, f32),
            pltpu.VMEM(items.shape, f32),
            pltpu.VMEM(item_state.shape, f32),
            pltpu.VMEM(positives.shape, jnp.int32),
            pltpu.VMEM((cols, 2 * TILE, width), bf16),
            pltpu.VMEM((STRATA, GROUPS, TILE, width), f32),
            pltpu.VMEM(items.shape, bf16),
            pltpu.VMEM((slots, block, TILE), bf16),
            pltpu.VMEM((slots, TILE, width), f32),
            pltpu.VMEM((STRATA, GROUPS, TILE, width), f32),
            pltpu.VMEM((STRATA, half, width), f32),
            pltpu.VMEM((STRATA, half, width), f32),
            pltpu.VMEM((STRATA, half, width), f32),
            pltpu.VMEM((STRATA, block, width), f32),
            pltpu.VMEM((STRATA, half, width), f32),
            pltpu.VMEM((half, width), f32),
            pltpu.VMEM((half, width), f32),
            pltpu.VMEM((half, width), f32),
            pltpu.VMEM((slots + 1, TILE, width), f32),
            pltpu.VMEM((slots + 1, TILE, width), f32),
            pltpu.VMEM((STRATA, slots, TILE, TILE), bf16),
            square, square, square, square, square, square,
            pltpu.VMEM((slots, 8, TILE), f32),
            pltpu.SMEM(ids.shape, jnp.int32),
            pltpu.SMEM(count.shape, jnp.int32),
            pltpu.SMEM(offsets.shape, jnp.int32),
            pltpu.SMEM((STRATA, tiles), jnp.int32),
            pltpu.SemaphoreType.DMA((2, 15, CHUNKS)),
            pltpu.SemaphoreType.DMA((len(arrays),)),
        ],
        compiler_params=pltpu.CompilerParams(
            collective_id=0, has_side_effects=True, vmem_limit_bytes=40 * 1024 * 1024
        ),
        name="whole",
    )(*[pltpu.with_memory_space_constraint(a, hbm) for a in arrays])
    return write_results(results)


def results_kernel(count, *refs):
    sems = refs[-1]
    copies = [
        pltpu.make_async_copy(refs[k], refs[count + k], sems.at[k]) for k in range(count)
    ]
    for copy in copies:
        copy.start()
    for copy in copies:
        copy.wait()


def write_results(arrays):
    count = len(arrays)
    return pl.pallas_call(
        functools.partial(results_kernel, count),
        out_shape=[jax.ShapeDtypeStruct(a.shape, a.dtype) for a in arrays],
        in_specs=[pl.BlockSpec(memory_space=VMEM)] * count,
        out_specs=[pl.BlockSpec(memory_space=pltpu.MemorySpace.HBM)] * count,
        scratch_shapes=[pltpu.SemaphoreType.DMA((count,))],
        compiler_params=pltpu.CompilerParams(vmem_limit_bytes=1024 * 1024),
        name="results",
    )(*arrays)


def passed_along(block, distance):
    size = lax.axis_size("wide")
    return lax.ppermute(block, "wide", [((i - distance) % size, i) for i in range(size)])


def general_exchange(shift, pos_grad, neg_grad, block, state):
    half = lax.axis_size("wide") // 2
    total = lax.psum(pos_grad + passed_along(neg_grad, half), "narrow")
    new_state = state + jnp.mean(total * total, axis=-1)
    block = block - step_rate * total / jnp.sqrt(new_state)[:, None]
    return passed_along((block, new_state), shift)


def per_device(users, user_state, items, item_state, tile_ids, tile_count, pos_items, neg_offsets):
    wide, narrow = lax.axis_size("wide"), lax.axis_size("narrow")
    ids, count = tile_ids[0, 0], tile_count[0]
    positives, offsets = pos_items[0, 0], neg_offsets[0, 0]
    own_state = user_state.reshape(-1, TILE)
    if narrow == 2:
        users, own_state, block, block_state = run_whole(
            users.reshape(-1, TILE, users.shape[1]), own_state, items, item_state.reshape(2, -1, TILE), ids, positives, count, offsets
        )
    else:
        block, block_state = items, item_state
        for stratum in range(STRATA):
            negatives = passed_along(block, wide // 2)
            users, own_state, pos_grad, neg_grad = run_tiles(
                stratum, ids, count, offsets, positives, users, own_state, block, negatives
            )
            shift = 1 - STRATA if stratum + 1 == STRATA else 1
            block, block_state = general_exchange(shift, pos_grad, neg_grad, block, block_state)
    return (users.reshape(-1, users.shape[-1]), own_state.reshape(user_state.shape), block, block_state.reshape(item_state.shape))


def solution(mesh):
    return jax.shard_map(
        per_device,
        mesh=mesh,
        in_specs=(
            P(("wide", "narrow"), None),
            P(("wide", "narrow")),
            P("wide", None),
            P("wide"),
            P("wide", "narrow", None, None),
            P("wide", "narrow", None),
            P("wide", "narrow", None, None, None),
            P("wide", "narrow", None, None),
        ),
        out_specs=(P(("wide", "narrow"), None), P(("wide", "narrow")), P("wide", None), P("wide")),
        check_vma=False,
    )
```

```python
import functools

import jax
import jax.numpy as jnp
from jax import lax
from jax.experimental import pallas as pl
from jax.experimental.pallas import tpu as pltpu
from jax.sharding import PartitionSpec as P

TILE = 128
STRATA = 2
BATCH = 4
GROUPS = 4
CHUNKS = 8
LAG_POS = 3
LAG_NEG = 4
ADD_FROM = (2, 3)
EARLY = 6
WINDOW = TILE + 16
MESH = pl.DeviceIdType.MESH
step_rate = 0.25
f32 = jnp.float32
bf16 = jnp.bfloat16
VMEM = pltpu.MemorySpace.VMEM
SMEM = pltpu.MemorySpace.SMEM


def dot(a, b, dims):
    return lax.dot_general(a, b, (dims, ((), ())), preferred_element_type=f32)


def pair(x):
    high = x.astype(bf16)
    low = (x - high.astype(f32)).astype(bf16)
    return jnp.concatenate([high, low], axis=0)


def tiles_kernel(
    stratum, ids, count, offsets, positives, users, state, block, negatives,
    new_users, new_state, pos_grad, neg_grad, split, square, padded, spread,
):
    cols = block.shape[0] // TILE
    rows = users.shape[0] // TILE
    side = TILE
    width = users.shape[1]
    new_users[...] = jnp.zeros(new_users.shape, f32)
    pos_grad[...] = jnp.zeros(pos_grad.shape, f32)
    spread[...] = jnp.zeros(spread.shape, f32)
    length = negatives.shape[0]
    padded[0:length, :] = negatives[...]
    padded[length:, :] = jnp.zeros((padded.shape[0] - length, width), f32)
    for col in range(cols):
        split[col] = pair(block[col * side : (col + 1) * side, :])
    live_count = count[0, stratum]
    item = lax.broadcasted_iota(jnp.int32, (side, side), 0)
    place = lax.broadcasted_iota(jnp.int32, (side, WINDOW), 1)

    def batch(step, carry):
        work = []
        for lane in range(BATCH):
            slot = step * BATCH + lane
            tile = ids[stratum, slot]
            within = lax.rem(offsets[stratum, slot], 8)
            window = pl.ds(pl.multiple_of(offsets[stratum, slot] - within, 8), WINDOW)
            row = pl.multiple_of(lax.div(tile, cols) * side, side)
            col = lax.rem(tile, cols)
            live = jnp.where(slot < live_count, 1.0 / side, 0.0).astype(f32)
            factors = users[pl.ds(row, side), :]
            factors_low = factors.astype(bf16)
            neg_rows = padded[window, :].astype(bf16)
            hot = jnp.where(item == positives[stratum, pl.ds(slot, 1), :], 1.0, 0.0).astype(f32)
            hot_t = hot.T.astype(bf16)
            hot = hot.astype(bf16)
            pos_rows = dot(jnp.concatenate([hot_t, hot_t], axis=1), split[col], ((1,), (0,)))
            neg_score = dot(factors_low, neg_rows, ((1,), (1,)))
            pos_score = jnp.sum(factors * pos_rows, axis=-1, keepdims=True)
            chosen = jnp.logical_and(place >= within, place < within + side)
            coeffs = jnp.where(chosen, live, 0.0) / (1.0 + jnp.exp(pos_score - neg_score))
            totals = jnp.sum(coeffs, axis=-1, keepdims=True)
            coeffs_low = coeffs.astype(bf16)
            factor_grad = dot(coeffs_low, neg_rows, ((1,), (0,))) - totals * pos_rows
            positive = dot(
                jnp.concatenate([hot, hot], axis=1), pair(totals * factors), ((1,), (0,))
            )
            coeffs_t = coeffs.T.astype(bf16)
            negative = dot(
                jnp.concatenate([coeffs_t, coeffs_t], axis=1), pair(factors), ((1,), (0,))
            )
            work.append((row, col, window, factor_grad, positive, negative))
        for row, col, window, factor_grad, positive, negative in work:
            new_users[pl.ds(row, side), :] += factor_grad
            at = pl.ds(pl.multiple_of(col * side, side), side)
            pos_grad[at, :] -= positive
            spread[window, :] += negative
        return carry

    lax.fori_loop(0, lax.div(live_count + (BATCH - 1), BATCH), batch, 0)
    neg_grad[...] = spread[0:length, :]
    square[...] = jnp.zeros(square.shape, f32)
    square[0:rows, :] = state[...]
    sums = square[...].T
    for row in range(rows):
        at = slice(row * side, (row + 1) * side)
        grad = new_users[at, :]
        fresh = sums[:, row : row + 1] + jnp.sum(grad * grad, axis=-1, keepdims=True) * (1.0 / width)
        new_users[at, :] = users[at, :] - (step_rate / jnp.sqrt(fresh)) * grad
        square[:, row : row + 1] = fresh
    new_state[...] = square[...].T[0:rows, :]


def run_tiles(stratum, ids, count, offsets, positives, users, state, block, negatives):
    width = users.shape[1]
    cols = block.shape[0] // TILE
    return pl.pallas_call(
        functools.partial(tiles_kernel, stratum),
        out_shape=(
            jax.ShapeDtypeStruct(users.shape, f32),
            jax.ShapeDtypeStruct(state.shape, f32),
            jax.ShapeDtypeStruct(block.shape, f32),
            jax.ShapeDtypeStruct(block.shape, f32),
        ),
        in_specs=[pl.BlockSpec(memory_space=SMEM)] * 3 + [pl.BlockSpec(memory_space=VMEM)] * 5,
        out_specs=(pl.BlockSpec(memory_space=VMEM),) * 4,
        scratch_shapes=[
            pltpu.VMEM((cols, 2 * TILE, width), bf16),
            pltpu.VMEM((TILE, TILE), f32),
            pltpu.VMEM((block.shape[0] + 16, width), f32),
            pltpu.VMEM((block.shape[0] + 16, width), f32),
        ],
        compiler_params=pltpu.CompilerParams(vmem_limit_bytes=24 * 1024 * 1024),
        name="tiles",
    )(ids, count, offsets, positives, users, state, block, negatives)


def greet(devices):
    barrier = pltpu.get_barrier_semaphore()
    for device in devices:
        pl.semaphore_signal(barrier, inc=1, device_id=device, device_id_type=MESH)
    pl.semaphore_wait(barrier, len(devices))


def start_remote(src, dst, sems, kind, chunk, device):
    copy = pltpu.make_async_remote_copy(
        src_ref=src,
        dst_ref=dst,
        send_sem=sems.at[0, kind, chunk],
        recv_sem=sems.at[1, kind, chunk],
        device_id=device,
        device_id_type=MESH,
    )
    copy.start()
    return copy


def whole_kernel(
    wide, users_hbm, user_state_hbm, items_hbm, item_state_hbm, ids_hbm, positives_hbm, count_hbm,
    offsets_hbm,
    new_users, new_user_state, new_items, new_item_state,
    users, high, low, user_state, block, block_next, item_state, positives, split, negs, negs_low,
    coeffs, pos_rows, neg_grad, beside_neg, summed, far, pos_grad, beside_pos, pos_sum, home_pos,
    fresh, factor_grad, pos_part, hot_t, square, columns, user_sums, item_sums, scores, totals, partial,
    ids, count, offsets, slot_of, sems, local_sems,
):
    w, r = lax.axis_index("wide"), lax.axis_index("narrow")
    slots = ids.shape[1]
    rows, side, width = users.shape
    cols = block.shape[0] // side
    half = block.shape[0] // 2
    size = half // CHUNKS
    per = CHUNKS // GROUPS
    quarter = half // GROUPS

    def at(shift):
        return (lax.rem(w + shift + wide, wide), r)

    across, ahead, behind = at(wide // 2), at(1), at(-1)
    far_ahead, far_behind = at(wide // 2 + 1), at(wide // 2 - 1)
    beside = (w, 1 - r)
    greet([beside, across, ahead, behind, far_ahead, far_behind])

    def span(which, chunk):
        return pl.ds(pl.multiple_of(which * half + chunk * size, size), size)

    def inner(which, chunk):
        return pl.ds(pl.multiple_of(which * quarter + (chunk % per) * size, size), size)

    def local(chunk):
        return slice(chunk * size, (chunk + 1) * size)

    started = []

    def send(src, dst, kind, chunk, device):
        copy = start_remote(src, dst, sems, kind, chunk, device)
        started.append(copy)
        return copy

    def neg_at(stratum, which, chunk):
        return negs.at[stratum, chunk // per, inner(which, chunk), :]

    arriving = [
        send(items_hbm.at[span(r, c), :], neg_at(0, r, c), 0, c, across) for c in range(CHUNKS)
    ]
    loads = []
    for k, (src, dst) in enumerate(
        [
            (ids_hbm, ids), (count_hbm, count), (offsets_hbm, offsets), (positives_hbm, positives),
            (items_hbm, block), (users_hbm, users), (user_state_hbm, user_state),
            (item_state_hbm, item_state),
        ]
    ):
        loads.append(pltpu.make_async_copy(src, dst, local_sems.at[k]))
        loads[-1].start()
    factor_grad[slots] = jnp.zeros((side, width), f32)
    pos_part[slots] = jnp.zeros((side, width), f32)
    columns[...] = jnp.zeros(columns.shape, f32)
    square[...] = jnp.zeros(square.shape, f32)
    for load in loads:
        load.wait()

    item = lax.broadcasted_iota(jnp.int32, (side, side), 0)

    def find(tile, carry):
        for stratum in range(STRATA):
            found = jnp.int32(slots)
            for slot in range(slots):
                found = jnp.where(ids[stratum, slot] == tile, jnp.int32(slot), found)
            slot_of[stratum, tile] = found
        return carry

    def hots(stratum):
        for slot in range(slots):
            hot = jnp.where(item == positives[stratum, slot : slot + 1, :], 1.0, 0.0).astype(f32)
            hot_t[stratum, slot] = hot.T.astype(bf16)

    def split_users(source):
        def step(row, carry):
            value = source[row]
            top = value.astype(bf16)
            high[row] = top
            low[row] = (value - top.astype(f32)).astype(bf16)
            return carry

        lax.fori_loop(0, rows, step, 0)

    def row_at(stratum, slot):
        return lax.div(ids[stratum, slot], cols)

    def prepare(stratum, source, own):
        for col in range(cols):
            split[col] = pair(own[col * side : (col + 1) * side, :])

        for slot in range(slots):
            hot = hot_t[stratum, slot]
            picked = dot(
                jnp.concatenate([hot, hot], axis=1),
                split[lax.rem(ids[stratum, slot], cols)],
                ((1,), (0,)),
            )
            pos_rows[slot] = picked
            columns[:, slot : slot + 1] = jnp.sum(
                source[row_at(stratum, slot)] * picked, axis=-1, keepdims=True
            )
        scores[...] = columns[...].T
        partial[...] = jnp.zeros(partial.shape, f32)

    def group(stratum, g):
        near = negs[stratum, g].astype(bf16)
        here = slice(g * side, (g + 1) * side)
        negs_low[here, :] = near
        index = item + jnp.where(item >= quarter, half - quarter, 0) + g * quarter

        weights, tops, lows = [], [], []
        for slot in range(slots):
            top = high[row_at(stratum, slot)]
            scale = jnp.where(slot < count[0, stratum], 0.5 / side, 0.0).astype(f32)
            score = dot(near, top, ((1,), (1,)))
            place = index - offsets[stratum, slot]
            chosen = jnp.logical_and(place >= 0, place < side)
            part = jnp.where(chosen, scale, 0.0)
            part += part * jnp.tanh(0.5 * (score - scores[slot : slot + 1, :]))
            partial[slot] += jnp.sum(part.reshape(side // 8, 8, side), axis=0)
            part = part.astype(bf16)
            coeffs[slot, here, :] = part
            weights.append(part)
            tops.append(top)
            lows.append(low[row_at(stratum, slot)])
        left = jnp.concatenate(weights, axis=1)
        neg_grad[stratum, g] = dot(left, jnp.concatenate(tops, axis=0), ((1,), (0,))) + dot(
            left, jnp.concatenate(lows, axis=0), ((1,), (0,))
        )

    def add_totals():
        square[0:slots, :] = jnp.sum(partial[...], axis=1)
        totals[...] = square[...].T

    def positive_part(stratum, slot):
        chosen = item == positives[stratum, slot : slot + 1, :]
        hot = jnp.where(chosen, square[slot : slot + 1, :], 0.0)
        top = hot.astype(bf16)
        rest = (hot - top.astype(f32)).astype(bf16)
        upper, lower = high[row_at(stratum, slot)], low[row_at(stratum, slot)]
        pos_part[slot] = dot(
            jnp.concatenate([top, rest], axis=1),
            jnp.concatenate([upper, upper], axis=0),
            ((1,), (0,)),
        ) + dot(top, lower, ((1,), (0,)))

    def positive(stratum, which):
        for k in range(cols // 2):
            col = which * (cols // 2) + k
            total = pos_part[slot_of[stratum, col]]
            for row in range(1, rows):
                total += pos_part[slot_of[stratum, row * cols + col]]
            pos_grad[stratum, pl.ds(pl.multiple_of(col * side, side), side), :] = -total

    def factor_part(slot):
        factor_grad[slot] = (
            dot(coeffs[slot], negs_low[...], ((0,), (0,)))
            - totals[:, slot : slot + 1] * pos_rows[slot]
        )

    def update_part(stratum, row, source, last):
        grad = factor_grad[slot_of[stratum, row * cols]]
        for col in range(1, cols):
            grad += factor_grad[slot_of[stratum, row * cols + col]]
        sums = user_sums[:, row : row + 1] + jnp.sum(grad * grad, axis=-1, keepdims=True) * (
            1.0 / width
        )
        value = source[row] - (step_rate / jnp.sqrt(sums)) * grad
        user_sums[:, row : row + 1] = sums
        new_users[row] = value
        if not last:
            top = value.astype(bf16)
            high[row] = top
            low[row] = (value - top.astype(f32)).astype(bf16)

    def user_work(stratum, source, last):
        for slot in range(slots):
            yield functools.partial(factor_part, slot)
        for row in range(rows):
            yield functools.partial(update_part, stratum, row, source, last)

    def adagrad(stratum, c, grad, value):
        col, begin = c * size // side, c * size % side
        sums = item_sums[begin : begin + size, col : col + 1] + jnp.sum(
            grad * grad, axis=-1, keepdims=True
        ) * (1.0 / width)
        item_sums[begin : begin + size, col : col + 1] = sums
        return value - (step_rate / jnp.sqrt(sums)) * grad

    square[0:rows, :] = user_state[...]
    user_sums[...] = square[...].T
    square[0 : half // side, :] = item_state[r]
    item_sums[...] = square[...].T
    hots(0)
    split_users(users)
    prepare(0, users, block)

    def chunks_of(g):
        return range(g * per, (g + 1) * per)

    def work_through(stratum, arriving, relayed, kind, target):
        side_neg, out = [], []

        def relay(c):
            arriving[c].wait_recv()
            relayed.append(send(neg_at(stratum, r, c), neg_at(stratum, r, c), kind, c, beside))

        def add(g):
            for c in chunks_of(g):
                side_neg[c].wait_recv()
                summed[stratum, local(c), :] = (
                    neg_grad[stratum, g, inner(r, c), :] + beside_neg[stratum, local(c), :]
                )
                out.append(
                    send(
                        summed.at[stratum, local(c), :], far.at[stratum, local(c), :],
                        kind + 2, c, target,
                    )
                )

        for g in range(GROUPS):
            for c in range(len(relayed), (g + 1) * per):
                relay(c)
            for c in chunks_of(g):
                relayed[c].wait_recv()
            if g + 1 < GROUPS:
                for c in range(len(relayed), (g + 2) * per):
                    relay(c)
            group(stratum, g)
            for c in chunks_of(g):
                side_neg.append(
                    send(
                        neg_grad.at[stratum, g, inner(1 - r, c), :],
                        beside_neg.at[stratum, local(c), :],
                        kind + 1, c, beside,
                    )
                )
            if g >= ADD_FROM[stratum]:
                add(g - ADD_FROM[stratum])
        add_totals()
        for slot in range(slots):
            positive_part(stratum, slot)
        positive(stratum, 1 - r)
        side_pos = [
            send(
                pos_grad.at[stratum, span(1 - r, c), :], beside_pos.at[stratum, local(c), :],
                kind + 3, c, beside,
            )
            for c in range(CHUNKS)
        ]
        for g in range(GROUPS - ADD_FROM[stratum], GROUPS):
            add(g)
        positive(stratum, r)
        return out, side_pos

    lax.fori_loop(0, rows * cols, find, 0)
    hots(1)
    out, side_pos = work_through(0, arriving, [], 1, across)
    work = list(user_work(0, users, False))
    pieces = CHUNKS + LAG_POS
    arriving, passed, relayed, shared = [], [], [], []
    for step in range(max(EARLY + LAG_NEG, CHUNKS + LAG_POS)):
        for piece in work[len(work) * step // pieces : len(work) * (step + 1) // pieces]:
            piece()
        if step < CHUNKS:
            c = step
            side_pos[c].wait_recv()
            out[c].wait_recv()
            grad = pos_grad[0, span(r, c), :] + beside_pos[0, local(c), :] + far[0, local(c), :]
            fresh[local(c), :] = adagrad(0, c, grad, block[span(r, c), :])
            arriving.append(send(fresh.at[local(c), :], neg_at(1, r, c), 5, c, far_ahead))
            passed.append(send(fresh.at[local(c), :], block_next.at[span(r, c), :], 6, c, ahead))
        if 0 <= step - LAG_POS < CHUNKS:
            c = step - LAG_POS
            passed[c].wait_recv()
            shared.append(
                send(block_next.at[span(r, c), :], block_next.at[span(r, c), :], 7, c, beside)
            )
        if 0 <= step - LAG_NEG < EARLY:
            c = step - LAG_NEG
            arriving[c].wait_recv()
            relayed.append(send(neg_at(1, r, c), neg_at(1, r, c), 8, c, beside))
    for c in range(CHUNKS):
        shared[c].wait_recv()
    prepare(1, new_users, block_next)
    out, side_pos = work_through(1, arriving, relayed, 8, far_behind)
    homeward, last = [], []
    work = list(user_work(1, new_users, True))
    steps = 2 * CHUNKS
    for step in range(steps):
        for piece in work[len(work) * step // CHUNKS : len(work) * (step + 1) // CHUNKS]:
            piece()
        c = step % CHUNKS
        if step < CHUNKS:
            side_pos[c].wait_recv()
            pos_sum[local(c), :] = pos_grad[1, span(r, c), :] + beside_pos[1, local(c), :]
            homeward.append(send(pos_sum.at[local(c), :], home_pos.at[local(c), :], 12, c, behind))
            if c == CHUNKS - 1:
                new_user_state[...] = user_sums[...].T[0:rows, :]
        else:
            homeward[c].wait_recv()
            out[c].wait_recv()
            grad = home_pos[local(c), :] + far[1, local(c), :]
            new_items[span(r, c), :] = adagrad(1, c, grad, fresh[local(c), :])
            here = new_items.at[span(r, c), :]
            last.append(send(here, here, 13, c, beside))
    new_item_state[r] = item_sums[...].T[0 : half // side, :]
    last.append(send(new_item_state.at[r], new_item_state.at[r], 14, 0, beside))
    for copy in last:
        copy.wait_recv()
    for copy in started:
        copy.wait_send()


def run_whole(users, user_state, items, item_state, ids, positives, count, offsets):
    block, width = items.shape
    half = block // 2
    slots = ids.shape[1]
    cols = block // TILE
    tiles = users.shape[0] * cols
    arrays = (users, user_state, items, item_state, ids, positives, count, offsets)
    hbm = pltpu.MemorySpace.HBM
    square = pltpu.VMEM((TILE, TILE), f32)
    results = pl.pallas_call(
        functools.partial(whole_kernel, lax.axis_size("wide")),
        out_shape=[jax.ShapeDtypeStruct(a.shape, f32) for a in arrays[:4]],
        in_specs=[pl.BlockSpec(memory_space=hbm)] * len(arrays),
        out_specs=[pl.BlockSpec(memory_space=VMEM)] * 4,
        scratch_shapes=[
            pltpu.VMEM(users.shape, f32),
            pltpu.VMEM(users.shape, bf16),
            pltpu.VMEM(users.shape, bf16),
            pltpu.VMEM(user_state.shape, f32),
            pltpu.VMEM(items.shape, f32),
            pltpu.VMEM(items.shape, f32),
            pltpu.VMEM(item_state.shape, f32),
            pltpu.VMEM(positives.shape, jnp.int32),
            pltpu.VMEM((cols, 2 * TILE, width), bf16),
            pltpu.VMEM((STRATA, GROUPS, TILE, width), f32),
            pltpu.VMEM(items.shape, bf16),
            pltpu.VMEM((slots, block, TILE), bf16),
            pltpu.VMEM((slots, TILE, width), f32),
            pltpu.VMEM((STRATA, GROUPS, TILE, width), f32),
            pltpu.VMEM((STRATA, half, width), f32),
            pltpu.VMEM((STRATA, half, width), f32),
            pltpu.VMEM((STRATA, half, width), f32),
            pltpu.VMEM((STRATA, block, width), f32),
            pltpu.VMEM((STRATA, half, width), f32),
            pltpu.VMEM((half, width), f32),
            pltpu.VMEM((half, width), f32),
            pltpu.VMEM((half, width), f32),
            pltpu.VMEM((slots + 1, TILE, width), f32),
            pltpu.VMEM((slots + 1, TILE, width), f32),
            pltpu.VMEM((STRATA, slots, TILE, TILE), bf16),
            square, square, square, square, square, square,
            pltpu.VMEM((slots, 8, TILE), f32),
            pltpu.SMEM(ids.shape, jnp.int32),
            pltpu.SMEM(count.shape, jnp.int32),
            pltpu.SMEM(offsets.shape, jnp.int32),
            pltpu.SMEM((STRATA, tiles), jnp.int32),
            pltpu.SemaphoreType.DMA((2, 15, CHUNKS)),
            pltpu.SemaphoreType.DMA((len(arrays),)),
        ],
        compiler_params=pltpu.CompilerParams(
            collective_id=0, has_side_effects=True, vmem_limit_bytes=40 * 1024 * 1024
        ),
        name="whole",
    )(*[pltpu.with_memory_space_constraint(a, hbm) for a in arrays])
    return write_results(results)


def results_kernel(count, *refs):
    sems = refs[-1]
    copies = [
        pltpu.make_async_copy(refs[k], refs[count + k], sems.at[k]) for k in range(count)
    ]
    for copy in copies:
        copy.start()
    for copy in copies:
        copy.wait()


def write_results(arrays):
    count = len(arrays)
    return pl.pallas_call(
        functools.partial(results_kernel, count),
        out_shape=[jax.ShapeDtypeStruct(a.shape, a.dtype) for a in arrays],
        in_specs=[pl.BlockSpec(memory_space=VMEM)] * count,
        out_specs=[pl.BlockSpec(memory_space=pltpu.MemorySpace.HBM)] * count,
        scratch_shapes=[pltpu.SemaphoreType.DMA((count,))],
        compiler_params=pltpu.CompilerParams(vmem_limit_bytes=1024 * 1024),
        name="results",
    )(*arrays)


def passed_along(block, distance):
    size = lax.axis_size("wide")
    return lax.ppermute(block, "wide", [((i - distance) % size, i) for i in range(size)])


def general_exchange(shift, pos_grad, neg_grad, block, state):
    half = lax.axis_size("wide") // 2
    total = lax.psum(pos_grad + passed_along(neg_grad, half), "narrow")
    new_state = state + jnp.mean(total * total, axis=-1)
    block = block - step_rate * total / jnp.sqrt(new_state)[:, None]
    return passed_along((block, new_state), shift)


def per_device(users, user_state, items, item_state, tile_ids, tile_count, pos_items, neg_offsets):
    wide, narrow = lax.axis_size("wide"), lax.axis_size("narrow")
    ids, count = tile_ids[0, 0], tile_count[0]
    positives, offsets = pos_items[0, 0], neg_offsets[0, 0]
    own_state = user_state.reshape(-1, TILE)
    if narrow == 2:
        users, own_state, block, block_state = run_whole(
            users.reshape(-1, TILE, users.shape[1]), own_state, items, item_state.reshape(2, -1, TILE), ids, positives, count, offsets
        )
    else:
        block, block_state = items, item_state
        for stratum in range(STRATA):
            negatives = passed_along(block, wide // 2)
            users, own_state, pos_grad, neg_grad = run_tiles(
                stratum, ids, count, offsets, positives, users, own_state, block, negatives
            )
            shift = 1 - STRATA if stratum + 1 == STRATA else 1
            block, block_state = general_exchange(shift, pos_grad, neg_grad, block, block_state)
    return (users.reshape(-1, users.shape[-1]), own_state.reshape(user_state.shape), block, block_state.reshape(item_state.shape))


def solution(mesh):
    return jax.shard_map(
        per_device,
        mesh=mesh,
        in_specs=(
            P(("wide", "narrow"), None),
            P(("wide", "narrow")),
            P("wide", None),
            P("wide"),
            P("wide", "narrow", None, None),
            P("wide", "narrow", None),
            P("wide", "narrow", None, None, None),
            P("wide", "narrow", None, None),
        ),
        out_specs=(P(("wide", "narrow"), None), P(("wide", "narrow")), P("wide", None), P("wide")),
        check_vma=False,
    )
```

```python
import functools

import jax
import jax.numpy as jnp
from jax import lax
from jax.experimental import pallas as pl
from jax.experimental.pallas import tpu as pltpu
from jax.sharding import PartitionSpec as P

TILE = 128
STRATA = 2
BATCH = 4
GROUPS = 4
CHUNKS = 8
LAG_POS = 3
LAG_NEG = 6
ADD_FROM = (2, 3)
EARLY = 8
WINDOW = TILE + 16
MESH = pl.DeviceIdType.MESH
step_rate = 0.25
f32 = jnp.float32
bf16 = jnp.bfloat16
VMEM = pltpu.MemorySpace.VMEM
SMEM = pltpu.MemorySpace.SMEM


def dot(a, b, dims):
    return lax.dot_general(a, b, (dims, ((), ())), preferred_element_type=f32)


def pair(x):
    high = x.astype(bf16)
    low = (x - high.astype(f32)).astype(bf16)
    return jnp.concatenate([high, low], axis=0)


def tiles_kernel(
    stratum, ids, count, offsets, positives, users, state, block, negatives,
    new_users, new_state, pos_grad, neg_grad, split, square, padded, spread,
):
    cols = block.shape[0] // TILE
    rows = users.shape[0] // TILE
    side = TILE
    width = users.shape[1]
    new_users[...] = jnp.zeros(new_users.shape, f32)
    pos_grad[...] = jnp.zeros(pos_grad.shape, f32)
    spread[...] = jnp.zeros(spread.shape, f32)
    length = negatives.shape[0]
    padded[0:length, :] = negatives[...]
    padded[length:, :] = jnp.zeros((padded.shape[0] - length, width), f32)
    for col in range(cols):
        split[col] = pair(block[col * side : (col + 1) * side, :])
    live_count = count[0, stratum]
    item = lax.broadcasted_iota(jnp.int32, (side, side), 0)
    place = lax.broadcasted_iota(jnp.int32, (side, WINDOW), 1)

    def batch(step, carry):
        work = []
        for lane in range(BATCH):
            slot = step * BATCH + lane
            tile = ids[stratum, slot]
            within = lax.rem(offsets[stratum, slot], 8)
            window = pl.ds(pl.multiple_of(offsets[stratum, slot] - within, 8), WINDOW)
            row = pl.multiple_of(lax.div(tile, cols) * side, side)
            col = lax.rem(tile, cols)
            live = jnp.where(slot < live_count, 1.0 / side, 0.0).astype(f32)
            factors = users[pl.ds(row, side), :]
            factors_low = factors.astype(bf16)
            neg_rows = padded[window, :].astype(bf16)
            hot = jnp.where(item == positives[stratum, pl.ds(slot, 1), :], 1.0, 0.0).astype(f32)
            hot_t = hot.T.astype(bf16)
            hot = hot.astype(bf16)
            pos_rows = dot(jnp.concatenate([hot_t, hot_t], axis=1), split[col], ((1,), (0,)))
            neg_score = dot(factors_low, neg_rows, ((1,), (1,)))
            pos_score = jnp.sum(factors * pos_rows, axis=-1, keepdims=True)
            chosen = jnp.logical_and(place >= within, place < within + side)
            coeffs = jnp.where(chosen, live, 0.0) / (1.0 + jnp.exp(pos_score - neg_score))
            totals = jnp.sum(coeffs, axis=-1, keepdims=True)
            coeffs_low = coeffs.astype(bf16)
            factor_grad = dot(coeffs_low, neg_rows, ((1,), (0,))) - totals * pos_rows
            positive = dot(
                jnp.concatenate([hot, hot], axis=1), pair(totals * factors), ((1,), (0,))
            )
            coeffs_t = coeffs.T.astype(bf16)
            negative = dot(
                jnp.concatenate([coeffs_t, coeffs_t], axis=1), pair(factors), ((1,), (0,))
            )
            work.append((row, col, window, factor_grad, positive, negative))
        for row, col, window, factor_grad, positive, negative in work:
            new_users[pl.ds(row, side), :] += factor_grad
            at = pl.ds(pl.multiple_of(col * side, side), side)
            pos_grad[at, :] -= positive
            spread[window, :] += negative
        return carry

    lax.fori_loop(0, lax.div(live_count + (BATCH - 1), BATCH), batch, 0)
    neg_grad[...] = spread[0:length, :]
    square[...] = jnp.zeros(square.shape, f32)
    square[0:rows, :] = state[...]
    sums = square[...].T
    for row in range(rows):
        at = slice(row * side, (row + 1) * side)
        grad = new_users[at, :]
        fresh = sums[:, row : row + 1] + jnp.sum(grad * grad, axis=-1, keepdims=True) * (1.0 / width)
        new_users[at, :] = users[at, :] - (step_rate / jnp.sqrt(fresh)) * grad
        square[:, row : row + 1] = fresh
    new_state[...] = square[...].T[0:rows, :]


def run_tiles(stratum, ids, count, offsets, positives, users, state, block, negatives):
    width = users.shape[1]
    cols = block.shape[0] // TILE
    return pl.pallas_call(
        functools.partial(tiles_kernel, stratum),
        out_shape=(
            jax.ShapeDtypeStruct(users.shape, f32),
            jax.ShapeDtypeStruct(state.shape, f32),
            jax.ShapeDtypeStruct(block.shape, f32),
            jax.ShapeDtypeStruct(block.shape, f32),
        ),
        in_specs=[pl.BlockSpec(memory_space=SMEM)] * 3 + [pl.BlockSpec(memory_space=VMEM)] * 5,
        out_specs=(pl.BlockSpec(memory_space=VMEM),) * 4,
        scratch_shapes=[
            pltpu.VMEM((cols, 2 * TILE, width), bf16),
            pltpu.VMEM((TILE, TILE), f32),
            pltpu.VMEM((block.shape[0] + 16, width), f32),
            pltpu.VMEM((block.shape[0] + 16, width), f32),
        ],
        compiler_params=pltpu.CompilerParams(vmem_limit_bytes=24 * 1024 * 1024),
        name="tiles",
    )(ids, count, offsets, positives, users, state, block, negatives)


def greet(devices):
    barrier = pltpu.get_barrier_semaphore()
    for device in devices:
        pl.semaphore_signal(barrier, inc=1, device_id=device, device_id_type=MESH)
    pl.semaphore_wait(barrier, len(devices))


def start_remote(src, dst, sems, kind, chunk, device):
    copy = pltpu.make_async_remote_copy(
        src_ref=src,
        dst_ref=dst,
        send_sem=sems.at[0, kind, chunk],
        recv_sem=sems.at[1, kind, chunk],
        device_id=device,
        device_id_type=MESH,
    )
    copy.start()
    return copy


def whole_kernel(
    wide, users_hbm, user_state_hbm, items_hbm, item_state_hbm, ids_hbm, positives_hbm, count_hbm,
    offsets_hbm,
    new_users, new_user_state, new_items, new_item_state,
    users, high, low, user_state, block, block_next, item_state, positives, split, negs, negs_low,
    coeffs, pos_rows, neg_grad, beside_neg, summed, far, pos_grad, beside_pos, pos_sum, home_pos,
    fresh, factor_grad, pos_part, hot_t, square, columns, user_sums, item_sums, scores, totals, partial,
    ids, count, offsets, slot_of, sems, local_sems,
):
    w, r = lax.axis_index("wide"), lax.axis_index("narrow")
    slots = ids.shape[1]
    rows, side, width = users.shape
    cols = block.shape[0] // side
    half = block.shape[0] // 2
    size = half // CHUNKS
    per = CHUNKS // GROUPS
    quarter = half // GROUPS

    def at(shift):
        return (lax.rem(w + shift + wide, wide), r)

    across, ahead, behind = at(wide // 2), at(1), at(-1)
    far_ahead, far_behind = at(wide // 2 + 1), at(wide // 2 - 1)
    beside = (w, 1 - r)
    greet([beside, across, ahead, behind, far_ahead, far_behind])

    def span(which, chunk):
        return pl.ds(pl.multiple_of(which * half + chunk * size, size), size)

    def inner(which, chunk):
        return pl.ds(pl.multiple_of(which * quarter + (chunk % per) * size, size), size)

    def local(chunk):
        return slice(chunk * size, (chunk + 1) * size)

    started = []

    def send(src, dst, kind, chunk, device):
        copy = start_remote(src, dst, sems, kind, chunk, device)
        started.append(copy)
        return copy

    def neg_at(stratum, which, chunk):
        return negs.at[stratum, chunk // per, inner(which, chunk), :]

    arriving = [
        send(items_hbm.at[span(r, c), :], neg_at(0, r, c), 0, c, across) for c in range(CHUNKS)
    ]
    loads = []
    for k, (src, dst) in enumerate(
        [
            (ids_hbm, ids), (count_hbm, count), (offsets_hbm, offsets), (positives_hbm, positives),
            (items_hbm, block), (users_hbm, users), (user_state_hbm, user_state),
            (item_state_hbm, item_state),
        ]
    ):
        loads.append(pltpu.make_async_copy(src, dst, local_sems.at[k]))
        loads[-1].start()
    factor_grad[slots] = jnp.zeros((side, width), f32)
    pos_part[slots] = jnp.zeros((side, width), f32)
    columns[...] = jnp.zeros(columns.shape, f32)
    square[...] = jnp.zeros(square.shape, f32)
    for load in loads:
        load.wait()

    item = lax.broadcasted_iota(jnp.int32, (side, side), 0)

    def find(tile, carry):
        for stratum in range(STRATA):
            found = jnp.int32(slots)
            for slot in range(slots):
                found = jnp.where(ids[stratum, slot] == tile, jnp.int32(slot), found)
            slot_of[stratum, tile] = found
        return carry

    def hots(stratum):
        for slot in range(slots):
            hot = jnp.where(item == positives[stratum, slot : slot + 1, :], 1.0, 0.0).astype(f32)
            hot_t[stratum, slot] = hot.T.astype(bf16)

    def split_users(source):
        def step(row, carry):
            value = source[row]
            top = value.astype(bf16)
            high[row] = top
            low[row] = (value - top.astype(f32)).astype(bf16)
            return carry

        lax.fori_loop(0, rows, step, 0)

    def row_at(stratum, slot):
        return lax.div(ids[stratum, slot], cols)

    def prepare(stratum, source, own):
        for col in range(cols):
            split[col] = pair(own[col * side : (col + 1) * side, :])

        for slot in range(slots):
            hot = hot_t[stratum, slot]
            picked = dot(
                jnp.concatenate([hot, hot], axis=1),
                split[lax.rem(ids[stratum, slot], cols)],
                ((1,), (0,)),
            )
            pos_rows[slot] = picked
            columns[:, slot : slot + 1] = jnp.sum(
                source[row_at(stratum, slot)] * picked, axis=-1, keepdims=True
            )
        scores[...] = columns[...].T
        partial[...] = jnp.zeros(partial.shape, f32)

    def group(stratum, g):
        near = negs[stratum, g].astype(bf16)
        here = slice(g * side, (g + 1) * side)
        negs_low[here, :] = near
        index = item + jnp.where(item >= quarter, half - quarter, 0) + g * quarter

        weights, tops, lows = [], [], []
        for slot in range(slots):
            top = high[row_at(stratum, slot)]
            scale = jnp.where(slot < count[0, stratum], 0.5 / side, 0.0).astype(f32)
            score = dot(near, top, ((1,), (1,)))
            place = index - offsets[stratum, slot]
            chosen = jnp.logical_and(place >= 0, place < side)
            part = jnp.where(chosen, scale, 0.0)
            part += part * jnp.tanh(0.5 * (score - scores[slot : slot + 1, :]))
            partial[slot] += jnp.sum(part.reshape(side // 8, 8, side), axis=0)
            part = part.astype(bf16)
            coeffs[slot, here, :] = part
            weights.append(part)
            tops.append(top)
            lows.append(low[row_at(stratum, slot)])
        left = jnp.concatenate(weights, axis=1)
        neg_grad[stratum, g] = dot(left, jnp.concatenate(tops, axis=0), ((1,), (0,))) + dot(
            left, jnp.concatenate(lows, axis=0), ((1,), (0,))
        )

    def add_totals():
        square[0:slots, :] = jnp.sum(partial[...], axis=1)
        totals[...] = square[...].T

    def positive_part(stratum, slot):
        chosen = item == positives[stratum, slot : slot + 1, :]
        hot = jnp.where(chosen, square[slot : slot + 1, :], 0.0)
        top = hot.astype(bf16)
        rest = (hot - top.astype(f32)).astype(bf16)
        upper, lower = high[row_at(stratum, slot)], low[row_at(stratum, slot)]
        pos_part[slot] = dot(
            jnp.concatenate([top, rest], axis=1),
            jnp.concatenate([upper, upper], axis=0),
            ((1,), (0,)),
        ) + dot(top, lower, ((1,), (0,)))

    def positive(stratum, which):
        for k in range(cols // 2):
            col = which * (cols // 2) + k
            total = pos_part[slot_of[stratum, col]]
            for row in range(1, rows):
                total += pos_part[slot_of[stratum, row * cols + col]]
            pos_grad[stratum, pl.ds(pl.multiple_of(col * side, side), side), :] = -total

    def factor_part(slot):
        factor_grad[slot] = (
            dot(coeffs[slot], negs_low[...], ((0,), (0,)))
            - totals[:, slot : slot + 1] * pos_rows[slot]
        )

    def update_part(stratum, row, source, last):
        grad = factor_grad[slot_of[stratum, row * cols]]
        for col in range(1, cols):
            grad += factor_grad[slot_of[stratum, row * cols + col]]
        sums = user_sums[:, row : row + 1] + jnp.sum(grad * grad, axis=-1, keepdims=True) * (
            1.0 / width
        )
        value = source[row] - (step_rate / jnp.sqrt(sums)) * grad
        user_sums[:, row : row + 1] = sums
        new_users[row] = value
        if not last:
            top = value.astype(bf16)
            high[row] = top
            low[row] = (value - top.astype(f32)).astype(bf16)

    def user_work(stratum, source, last):
        for slot in range(slots):
            yield functools.partial(factor_part, slot)
        for row in range(rows):
            yield functools.partial(update_part, stratum, row, source, last)

    def adagrad(stratum, c, grad, value):
        col, begin = c * size // side, c * size % side
        sums = item_sums[begin : begin + size, col : col + 1] + jnp.sum(
            grad * grad, axis=-1, keepdims=True
        ) * (1.0 / width)
        item_sums[begin : begin + size, col : col + 1] = sums
        return value - (step_rate / jnp.sqrt(sums)) * grad

    square[0:rows, :] = user_state[...]
    user_sums[...] = square[...].T
    square[0 : half // side, :] = item_state[r]
    item_sums[...] = square[...].T
    hots(0)
    split_users(users)
    prepare(0, users, block)

    def chunks_of(g):
        return range(g * per, (g + 1) * per)

    def work_through(stratum, arriving, relayed, kind, target):
        side_neg, out = [], []

        def relay(c):
            arriving[c].wait_recv()
            relayed.append(send(neg_at(stratum, r, c), neg_at(stratum, r, c), kind, c, beside))

        def add(g):
            for c in chunks_of(g):
                side_neg[c].wait_recv()
                summed[stratum, local(c), :] = (
                    neg_grad[stratum, g, inner(r, c), :] + beside_neg[stratum, local(c), :]
                )
                out.append(
                    send(
                        summed.at[stratum, local(c), :], far.at[stratum, local(c), :],
                        kind + 2, c, target,
                    )
                )

        for g in range(GROUPS):
            for c in range(len(relayed), (g + 1) * per):
                relay(c)
            for c in chunks_of(g):
                relayed[c].wait_recv()
            if g + 1 < GROUPS:
                for c in range(len(relayed), (g + 2) * per):
                    relay(c)
            group(stratum, g)
            for c in chunks_of(g):
                side_neg.append(
                    send(
                        neg_grad.at[stratum, g, inner(1 - r, c), :],
                        beside_neg.at[stratum, local(c), :],
                        kind + 1, c, beside,
                    )
                )
            if g >= ADD_FROM[stratum]:
                add(g - ADD_FROM[stratum])
        add_totals()
        for slot in range(slots):
            positive_part(stratum, slot)
        positive(stratum, 1 - r)
        side_pos = [
            send(
                pos_grad.at[stratum, span(1 - r, c), :], beside_pos.at[stratum, local(c), :],
                kind + 3, c, beside,
            )
            for c in range(CHUNKS)
        ]
        for g in range(GROUPS - ADD_FROM[stratum], GROUPS):
            add(g)
        positive(stratum, r)
        return out, side_pos

    lax.fori_loop(0, rows * cols, find, 0)
    hots(1)
    out, side_pos = work_through(0, arriving, [], 1, across)
    work = list(user_work(0, users, False))
    pieces = CHUNKS + LAG_POS
    arriving, passed, relayed, shared = [], [], [], []
    for step in range(EARLY + LAG_NEG):
        for piece in work[len(work) * step // pieces : len(work) * (step + 1) // pieces]:
            piece()
        if step < CHUNKS:
            c = step
            side_pos[c].wait_recv()
            out[c].wait_recv()
            grad = pos_grad[0, span(r, c), :] + beside_pos[0, local(c), :] + far[0, local(c), :]
            fresh[local(c), :] = adagrad(0, c, grad, block[span(r, c), :])
            passed.append(send(fresh.at[local(c), :], block_next.at[span(r, c), :], 6, c, ahead))
            arriving.append(send(fresh.at[local(c), :], neg_at(1, r, c), 5, c, far_ahead))
        if 0 <= step - LAG_POS < CHUNKS:
            c = step - LAG_POS
            passed[c].wait_recv()
            shared.append(
                send(block_next.at[span(r, c), :], block_next.at[span(r, c), :], 7, c, beside)
            )
        if 0 <= step - LAG_NEG < EARLY:
            c = step - LAG_NEG
            arriving[c].wait_recv()
            relayed.append(send(neg_at(1, r, c), neg_at(1, r, c), 8, c, beside))
    for c in range(CHUNKS):
        shared[c].wait_recv()
    prepare(1, new_users, block_next)
    out, side_pos = work_through(1, arriving, relayed, 8, far_behind)
    homeward, last = [], []
    work = list(user_work(1, new_users, True))
    steps = 2 * CHUNKS
    for step in range(steps):
        for piece in work[len(work) * step // CHUNKS : len(work) * (step + 1) // CHUNKS]:
            piece()
        c = step % CHUNKS
        if step < CHUNKS:
            side_pos[c].wait_recv()
            pos_sum[local(c), :] = pos_grad[1, span(r, c), :] + beside_pos[1, local(c), :]
            homeward.append(send(pos_sum.at[local(c), :], home_pos.at[local(c), :], 12, c, behind))
            if c == CHUNKS - 1:
                new_user_state[...] = user_sums[...].T[0:rows, :]
        else:
            homeward[c].wait_recv()
            out[c].wait_recv()
            grad = home_pos[local(c), :] + far[1, local(c), :]
            new_items[span(r, c), :] = adagrad(1, c, grad, fresh[local(c), :])
            here = new_items.at[span(r, c), :]
            last.append(send(here, here, 13, c, beside))
    new_item_state[r] = item_sums[...].T[0 : half // side, :]
    last.append(send(new_item_state.at[r], new_item_state.at[r], 14, 0, beside))
    for copy in last:
        copy.wait_recv()
    for copy in started:
        copy.wait_send()


def run_whole(users, user_state, items, item_state, ids, positives, count, offsets):
    block, width = items.shape
    half = block // 2
    slots = ids.shape[1]
    cols = block // TILE
    tiles = users.shape[0] * cols
    arrays = (users, user_state, items, item_state, ids, positives, count, offsets)
    hbm = pltpu.MemorySpace.HBM
    square = pltpu.VMEM((TILE, TILE), f32)
    results = pl.pallas_call(
        functools.partial(whole_kernel, lax.axis_size("wide")),
        out_shape=[jax.ShapeDtypeStruct(a.shape, f32) for a in arrays[:4]],
        in_specs=[pl.BlockSpec(memory_space=hbm)] * len(arrays),
        out_specs=[pl.BlockSpec(memory_space=VMEM)] * 4,
        scratch_shapes=[
            pltpu.VMEM(users.shape, f32),
            pltpu.VMEM(users.shape, bf16),
            pltpu.VMEM(users.shape, bf16),
            pltpu.VMEM(user_state.shape, f32),
            pltpu.VMEM(items.shape, f32),
            pltpu.VMEM(items.shape, f32),
            pltpu.VMEM(item_state.shape, f32),
            pltpu.VMEM(positives.shape, jnp.int32),
            pltpu.VMEM((cols, 2 * TILE, width), bf16),
            pltpu.VMEM((STRATA, GROUPS, TILE, width), f32),
            pltpu.VMEM(items.shape, bf16),
            pltpu.VMEM((slots, block, TILE), bf16),
            pltpu.VMEM((slots, TILE, width), f32),
            pltpu.VMEM((STRATA, GROUPS, TILE, width), f32),
            pltpu.VMEM((STRATA, half, width), f32),
            pltpu.VMEM((STRATA, half, width), f32),
            pltpu.VMEM((STRATA, half, width), f32),
            pltpu.VMEM((STRATA, block, width), f32),
            pltpu.VMEM((STRATA, half, width), f32),
            pltpu.VMEM((half, width), f32),
            pltpu.VMEM((half, width), f32),
            pltpu.VMEM((half, width), f32),
            pltpu.VMEM((slots + 1, TILE, width), f32),
            pltpu.VMEM((slots + 1, TILE, width), f32),
            pltpu.VMEM((STRATA, slots, TILE, TILE), bf16),
            square, square, square, square, square, square,
            pltpu.VMEM((slots, 8, TILE), f32),
            pltpu.SMEM(ids.shape, jnp.int32),
            pltpu.SMEM(count.shape, jnp.int32),
            pltpu.SMEM(offsets.shape, jnp.int32),
            pltpu.SMEM((STRATA, tiles), jnp.int32),
            pltpu.SemaphoreType.DMA((2, 15, CHUNKS)),
            pltpu.SemaphoreType.DMA((len(arrays),)),
        ],
        compiler_params=pltpu.CompilerParams(
            collective_id=0, has_side_effects=True, vmem_limit_bytes=40 * 1024 * 1024
        ),
        name="whole",
    )(*[pltpu.with_memory_space_constraint(a, hbm) for a in arrays])
    return write_results(results)


def results_kernel(count, *refs):
    sems = refs[-1]
    copies = [
        pltpu.make_async_copy(refs[k], refs[count + k], sems.at[k]) for k in range(count)
    ]
    for copy in copies:
        copy.start()
    for copy in copies:
        copy.wait()


def write_results(arrays):
    count = len(arrays)
    return pl.pallas_call(
        functools.partial(results_kernel, count),
        out_shape=[jax.ShapeDtypeStruct(a.shape, a.dtype) for a in arrays],
        in_specs=[pl.BlockSpec(memory_space=VMEM)] * count,
        out_specs=[pl.BlockSpec(memory_space=pltpu.MemorySpace.HBM)] * count,
        scratch_shapes=[pltpu.SemaphoreType.DMA((count,))],
        compiler_params=pltpu.CompilerParams(vmem_limit_bytes=1024 * 1024),
        name="results",
    )(*arrays)


def passed_along(block, distance):
    size = lax.axis_size("wide")
    return lax.ppermute(block, "wide", [((i - distance) % size, i) for i in range(size)])


def general_exchange(shift, pos_grad, neg_grad, block, state):
    half = lax.axis_size("wide") // 2
    total = lax.psum(pos_grad + passed_along(neg_grad, half), "narrow")
    new_state = state + jnp.mean(total * total, axis=-1)
    block = block - step_rate * total / jnp.sqrt(new_state)[:, None]
    return passed_along((block, new_state), shift)


def per_device(users, user_state, items, item_state, tile_ids, tile_count, pos_items, neg_offsets):
    wide, narrow = lax.axis_size("wide"), lax.axis_size("narrow")
    ids, count = tile_ids[0, 0], tile_count[0]
    positives, offsets = pos_items[0, 0], neg_offsets[0, 0]
    own_state = user_state.reshape(-1, TILE)
    if narrow == 2:
        users, own_state, block, block_state = run_whole(
            users.reshape(-1, TILE, users.shape[1]), own_state, items, item_state.reshape(2, -1, TILE), ids, positives, count, offsets
        )
    else:
        block, block_state = items, item_state
        for stratum in range(STRATA):
            negatives = passed_along(block, wide // 2)
            users, own_state, pos_grad, neg_grad = run_tiles(
                stratum, ids, count, offsets, positives, users, own_state, block, negatives
            )
            shift = 1 - STRATA if stratum + 1 == STRATA else 1
            block, block_state = general_exchange(shift, pos_grad, neg_grad, block, block_state)
    return (users.reshape(-1, users.shape[-1]), own_state.reshape(user_state.shape), block, block_state.reshape(item_state.shape))


def solution(mesh):
    return jax.shard_map(
        per_device,
        mesh=mesh,
        in_specs=(
            P(("wide", "narrow"), None),
            P(("wide", "narrow")),
            P("wide", None),
            P("wide"),
            P("wide", "narrow", None, None),
            P("wide", "narrow", None),
            P("wide", "narrow", None, None, None),
            P("wide", "narrow", None, None),
        ),
        out_specs=(P(("wide", "narrow"), None), P(("wide", "narrow")), P("wide", None), P("wide")),
        check_vma=False,
    )
```
